32 devices in a mesh: orb: 4 (over y, x), grid: 8 (over z, core).
Axes of the slice: x: 2, y: 2, z: 4, core: 2. Of those that a mesh axis runs over, the one named last changes fastest.
Arguments:
- orbitals: float32 [4, 96, 192, 256], P('orb', 'grid'), may hold values from -6 to 6
- potential: float32 [96, 192, 256], P('grid'), may hold values from -4 to 0
- trial_potential: float32 [96, 192, 256], P('grid'), may hold values from -6 to 6
- eigenvalues: float32 [4], P('orb'), may hold values from -3 to 0
- frequency: float32 [1], replicated, may hold values from 1 to 8
Outputs:
- solutions: float32 [4, 96, 192, 256], P('orb', 'grid')
- density: float32 [96, 192, 256], P('grid', 'orb')
The draws below stay inside these ranges and needn't reach their ends.
All inputs are finite; a program needn't handle non-finite values.
Results may differ from the reference program's by a relative error of at most 0.0001.
Values sent between devices are 32-bit elements; how exact they have to be, the bound alone decides.
A program may use at most 192 MiB of HBM per device.

```python
import math
import jax
import jax.numpy as jnp
from jax import lax

NY = 192
NZ = 256
ITERS = 2
NORB = 4
NX = 96


def level_of(stream_key, dims, cuts, low, top_value):
    factor_of = 1.0
    for position, blocks in cuts:
        heights = jax.random.uniform(jax.random.fold_in(jax.random.fold_in(stream_key, 6), position), (blocks,), jnp.float32, low / len(cuts), top_value / len(cuts))
        factor_of = factor_of * jnp.repeat(jnp.exp(heights), dims[position] // blocks).reshape((-1,) + (1,) * (len(dims) - 1 - position))
    return factor_of


def gaussian(own_key, shape, scale, most, split=(), kind=jnp.bfloat16):
    array = jax.random.normal(own_key, shape, jnp.float32) * scale
    if len(split) > 0:
        array = level_of(own_key, shape, split, -0.22, 0.18) * array
    return jnp.clip(array, min=-most, max=most).astype(kind)


def setup_inputs(seed: int = 0) -> dict:
    key_list = jax.random.split(jax.random.key(seed), 6)
    return {
        "orbitals": gaussian(key_list[0], (NORB, NX, NY, NZ), 1.0, 6.0, ((0, 4), (1, 8)), jnp.float32),
        "potential": jnp.clip(-4.0 + 4.0 * jax.random.uniform(key_list[1], (NX, NY, NZ), jnp.float32) ** level_of(key_list[1], (NX, NY, NZ), ((0, 8),), -0.2, 0.2), -4.0, 0.0),
        "trial_potential": gaussian(key_list[2], (NX, NY, NZ), 1.0, 6.0, ((0, 8),), jnp.float32),
        "eigenvalues": jnp.clip(-3.0 + 3.0 * jax.random.uniform(key_list[3], (NORB,), jnp.float32) ** level_of(key_list[3], (NORB,), ((0, 4),), -0.2, 0.2), -3.0, 0.0),
        "frequency": jnp.clip(jnp.exp(jax.random.uniform(key_list[4], (1,), jnp.float32, math.log(1.0), math.log(8.0))), 1.0, 8.0),
    }


STENCIL = (-5369.0 / 1800.0, 12.0 / 7.0, -15.0 / 56.0, 10.0 / 189.0, -1.0 / 112.0, 2.0 / 1925.0, -1.0 / 16632.0)
SPACING = 0.75


def shifted_hamiltonian(padded, potential, energy):
    axis_rows = padded.ndim - 3
    axis_cols = padded.ndim - 2
    length = padded.shape[axis_rows] - 12
    width = padded.shape[axis_cols]
    wrapped = jnp.concatenate([padded[..., width - 6:, :], padded, padded[..., :6, :]], axis=axis_cols)

    def take(row_off, col_off):
        part = lax.slice_in_dim(wrapped, 6 + row_off, 6 + row_off + length, axis=axis_rows)
        return lax.slice_in_dim(part, 6 + col_off, 6 + col_off + width, axis=axis_cols)

    center = take(0, 0)
    summed = 3.0 * STENCIL[0] * center
    for offset in range(1, 7):
        beside_all = take(offset, 0) + take(-offset, 0) + take(0, offset) + take(0, -offset)
        beside_all = beside_all + jnp.roll(center, offset, -1) + jnp.roll(center, -offset, -1)
        summed = summed + STENCIL[offset] * beside_all
    return (-0.5 / (SPACING * SPACING)) * summed + (potential - energy) * center


def pad_rows(field):
    return jnp.pad(field, ((6, 6), (0, 0), (0, 0)))


def reference(orbitals, potential, trial_potential, eigenvalues, frequency):
    squared = frequency[0] * frequency[0]

    def solve_one(item):
        orbital, energy = item

        def shifted(field):
            return shifted_hamiltonian(pad_rows(field), potential, energy)

        def operator(field):
            return shifted(shifted(field)) + squared * field

        source = trial_potential * orbital
        solution = jnp.zeros_like(source)
        residual = source
        direction = source
        norm_now = jnp.sum(residual * residual)
        for step in range(ITERS):
            image = operator(direction)
            step_size = norm_now / jnp.sum(direction * image)
            solution = solution + step_size * direction
            residual = residual - step_size * image
            norm_next = jnp.sum(residual * residual)
            direction = residual + (norm_next / norm_now) * direction
            norm_now = norm_next
        response = -4.0 * orbital * shifted(solution)
        return solution, response

    solutions, responses = lax.map(solve_one, (orbitals, eigenvalues))
    return solutions, jnp.sum(responses, axis=0)
```

```python
import functools

import jax
import jax.numpy as jnp
from jax import lax
from jax.experimental import pallas as pl
from jax.experimental.pallas import tpu as pltpu
from jax.sharding import PartitionSpec as P

STENCIL = (
    -5369.0 / 1800.0,
    12.0 / 7.0,
    -15.0 / 56.0,
    10.0 / 189.0,
    -1.0 / 112.0,
    2.0 / 1925.0,
    -1.0 / 16632.0,
)
SPACING = 0.75
REACH = len(STENCIL) - 1
COEFS = tuple(-0.5 / (SPACING * SPACING) * c for c in STENCIL)
STRIP = 8


def circulant(ref, count):
    size = ref.shape[1]

    def step(s, carry):
        rows = pl.ds(pl.multiple_of(s * count, count), count)
        row = s * count + lax.broadcasted_iota(jnp.int32, (count, size), 0)
        apart = jnp.abs(row - lax.broadcasted_iota(jnp.int32, (count, size), 1))
        apart = jnp.minimum(apart, size - apart)
        full = jnp.zeros((count, size), jnp.float32)
        for k in range(1, REACH + 1):
            full = jnp.where(apart == k, COEFS[k], full)
        high = full.astype(jnp.bfloat16)
        ref[0, rows, :] = high
        ref[1, rows, :] = (full - high.astype(jnp.float32)).astype(jnp.bfloat16)
        return carry

    lax.fori_loop(0, size // count, step, 0)


def kernel(
    n,
    orb_hbm, pot_hbm, tri_hbm, eig_hbm, freq_hbm,
    src, dens,
    orb, pot, tri, img, two, fin, cz, cy,
    hslow, hfast, sums, ship, land, ship_late, land_late, mix,
    eig, freq, ld_sem, mat_sem,
    slow_s, slow_r, fast_s, fast_r, sum_s, sum_r,
    ship_s, ship_r, late_s, late_r, mix_s, mix_r,
):
    planes, ny, nz = src.shape
    wide = 32
    late = ship_late.shape[1]
    quarter = ship.shape[3]
    g = lax.axis_index("grid")
    o = lax.axis_index("orb")
    odd = lax.rem(g, 2)
    slow_id = lax.rem(g + n - 1 + 2 * odd, n)
    fast_id = g + 1 - 2 * odd
    has_slow = jnp.logical_and(g + odd > 0, g + odd < n)
    flip1 = o + 1 - 2 * lax.rem(o, 2)
    flip2 = lax.rem(o + 2, 4)
    first = (1 - odd) * flip1 + odd * flip2
    second = odd * flip1 + (1 - odd) * flip2
    both = 3 - o
    quarters = (both, first, second, o)

    barrier = pltpu.get_barrier_semaphore()
    for j in range(1, n):
        pl.semaphore_signal(barrier, inc=1, device_id={"grid": lax.rem(g + j, n)})
    for slot in range(3):
        pl.semaphore_signal(barrier, inc=1, device_id={"orb": quarters[slot]})

    def at(d):
        return d + odd * (planes - 1 - 2 * d)

    def span(d, count):
        return pl.ds(d + odd * (planes - count - 2 * d), count)

    def load(which, d):
        hbm, ref = ((orb_hbm, orb), (tri_hbm, tri))[which]
        return pltpu.make_async_copy(hbm.at[at(d)], ref.at[at(d)], ld_sem.at[which, d])

    order = list(range(REACH)) + list(range(planes - 1, REACH - 1, -1))
    for d in order:
        load(0, d).start()
        load(1, d).start()
    mats = [
        pltpu.make_async_copy(pot_hbm, pot, mat_sem.at[0]),
        pltpu.make_async_copy(eig_hbm, eig, mat_sem.at[1]),
        pltpu.make_async_copy(freq_hbm, freq, mat_sem.at[2]),
    ]
    for copy in mats:
        copy.start()

    fields = (src, img, two)

    def slow(r, k):
        return pltpu.make_async_remote_copy(
            src_ref=fields[r].at[at(k)], dst_ref=hslow.at[r, k],
            send_sem=slow_s.at[r], recv_sem=slow_r.at[r, k],
            device_id={"grid": slow_id}, device_id_type=pl.DeviceIdType.MESH)

    def slow_sent(r):
        return pltpu.make_async_remote_copy(
            src_ref=fields[r].at[span(0, REACH)], dst_ref=hslow.at[r],
            send_sem=slow_s.at[r], recv_sem=slow_r.at[r, 0],
            device_id={"grid": slow_id}, device_id_type=pl.DeviceIdType.MESH)

    def fast(r):
        return pltpu.make_async_remote_copy(
            src_ref=fields[r].at[span(planes - REACH, REACH)], dst_ref=hfast.at[r],
            send_sem=fast_s.at[r], recv_sem=fast_r.at[r],
            device_id={"grid": fast_id}, device_id_type=pl.DeviceIdType.MESH)

    def send(r, *ks):
        @pl.when(has_slow)
        def _():
            for k in ks:
                slow(r, k).start()

    def rows_in(slot):
        return pl.ds(pl.multiple_of(quarters[slot] * quarter, 8), quarter)

    def rows_of(s, count):
        return pl.ds(pl.multiple_of(s * count, count), count)

    def over(step, init, count=wide):
        return lax.fori_loop(0, ny // count, step, init)

    def ship_copy(field, slot, d, count, sem):
        piece = pl.ds(d - late, count)
        return pltpu.make_async_remote_copy(
            src_ref=ship.at[field, slot, piece], dst_ref=land.at[field, slot, piece],
            send_sem=ship_s, recv_sem=ship_r.at[field, slot, sem],
            device_id={"orb": quarters[slot]}, device_id_type=pl.DeviceIdType.MESH)

    batches = (
        ((REACH, planes - REACH), (late, REACH - late)),
        ((REACH, planes - REACH),) + tuple((d, 1) for d in range(REACH - 1, late - 1, -1)),
    )

    def share(field, value, batch):
        d, count = batches[field][batch]
        for slot in range(3):
            rows = rows_in(slot)
            for e in range(d, d + count):
                ship[field, slot, e - late] = orb[at(e), rows, :] * value[at(e), rows, :]
            ship_copy(field, slot, d, count, batch).start()

    zero = jnp.zeros((wide, nz), jnp.float32)

    def arrive(r, ks, acc):
        @pl.when(has_slow)
        def _():
            for k in ks:
                slow(r, k).wait_recv()

            def step(s, carry):
                rows = rows_of(s, wide)
                values = [hslow[r, k, rows, :] for k in ks]
                for d in range(REACH):
                    terms = [COEFS[d + 1 + k] * v for k, v in zip(ks, values) if d + k < REACH]
                    if terms:
                        acc[at(d), rows, :] = acc[at(d), rows, :] + functools.reduce(jnp.add, terms)
                return carry

            over(step, 0)

    def square_of(ref, d, total):
        def step(s, carry):
            value = ref[at(d), rows_of(s, wide), :]
            return carry + value * value

        return over(step, total)

    def across(value, out, low, high):
        def plane(d, carry):
            p = at(d)
            whole = value[p]
            high_part = whole.astype(jnp.bfloat16)
            low_part = (whole - high_part.astype(jnp.float32)).astype(jnp.bfloat16)
            product = functools.partial(jnp.dot, preferred_element_type=jnp.float32)
            along_z = product(high_part, cz[0]) + product(low_part, cz[0]) + product(high_part, cz[1])
            along_y = product(cy[0], high_part) + product(cy[0], low_part) + product(cy[1], high_part)
            out[p] = along_z + along_y
            return carry

        lax.fori_loop(low, high, plane, 0)

    def along(r, value, out):
        fast(r).wait_recv()

        def strip(s, carry):
            rows = rows_of(s, STRIP)
            parts = [value[at(d), rows, :] for d in range(planes)]
            parts += [hfast[r, k + odd * (REACH - 1 - 2 * k), rows, :] for k in range(REACH)]
            for d in range(planes):
                total = out[at(d), rows, :] + (pot[at(d), rows, :] + (3.0 * COEFS[0] - energy)) * parts[d]
                for k in range(1, REACH + 1):
                    near = [parts[e] for e in (d - k, d + k) if 0 <= e < planes + REACH]
                    total = total + COEFS[k] * (near[0] + near[1] if len(near) == 2 else near[0])
                out[at(d), rows, :] = total
            return carry

        over(strip, 0, STRIP)

    def fold(total):
        total = functools.reduce(
            lambda a, b: a + b, [total[i:i + 8] for i in range(0, wide, 8)])
        total = functools.reduce(
            lambda a, b: a + b, [total[:, i:i + 128] for i in range(0, nz, 128)])
        return jnp.sum(total, axis=0, keepdims=True)

    def exchange(r, j, slot):
        return pltpu.make_async_remote_copy(
            src_ref=sums.at[r, slot], dst_ref=sums.at[r, slot],
            send_sem=sum_s.at[r], recv_sem=sum_r.at[r],
            device_id={"grid": lax.rem(g + j, n)}, device_id_type=pl.DeviceIdType.MESH)

    def exchanged(r):
        return pltpu.make_async_remote_copy(
            src_ref=sums.at[r, pl.ds(0, n - 1)], dst_ref=sums.at[r, pl.ds(0, n - 1)],
            send_sem=sum_s.at[r], recv_sem=sum_r.at[r],
            device_id={"grid": fast_id}, device_id_type=pl.DeviceIdType.MESH)

    def post(r, *totals):
        for i in range(2):
            row = fold(totals[i]) if i < len(totals) else jnp.zeros((1, 128), jnp.float32)
            sums[r, g, i:i + 1, :] = row
        for j in range(1, n):
            exchange(r, j, g).start()

    def collect(r):
        exchanged(r).wait_recv()
        total = sums[r, 0]
        for m in range(1, n):
            total = total + sums[r, m]
        return tuple(jnp.sum(total[i:i + 1], keepdims=True) for i in range(2))

    def spread(value):
        return jnp.broadcast_to(value, (1, nz))

    circulant(cz, 32)
    circulant(cy, 32)

    total_src = zero
    for d in order:
        load(0, d).wait()
        load(1, d).wait()

        def step(s, carry, d=d):
            rows = rows_of(s, wide)
            value = orb[at(d), rows, :] * tri[at(d), rows, :]
            src[at(d), rows, :] = value
            return carry + value * value

        total_src = over(step, total_src)
        if d == order[0]:
            pl.semaphore_wait(barrier, n + 2)
        if d < REACH:
            send(0, d)
    fast(0).start()
    for copy in mats:
        copy.wait()
    energy = eig[0]
    squared = freq[0] * freq[0]

    across(src, img, 0, planes)
    along(0, src, img)
    fast(1).start()
    share(0, img, 0)
    total_img = zero
    for d in range(REACH, planes):
        total_img = square_of(img, d, total_img)
    early = list(range(REACH - late))
    arrive(0, early, img)
    send(1, REACH - 1)
    share(0, img, 1)
    for k in early:
        total_img = square_of(img, REACH - 1 - k, total_img)
    across(img, two, late, planes)
    for k in range(REACH - late, REACH):
        arrive(0, [k], img)
        total_img = square_of(img, REACH - 1 - k, total_img)
        if k < REACH - 1:
            across(img, two, REACH - 1 - k, REACH - k)
    post(0, total_src, total_img)
    send(1, *range(REACH - 1))
    across(img, two, 0, 1)
    along(1, img, two)
    fast(2).start()

    across(two, fin, REACH, planes)
    arrive(1, [REACH - 1, 0], two)
    send(2, REACH - 1)
    across(two, fin, REACH - 1, REACH)
    norm0, form0 = collect(0)
    step0 = norm0 / (form0 + squared * norm0)
    back = spread(1.0 - step0 * squared)
    step0_row = spread(step0)

    def square_res(d, total):
        def step(s, carry):
            rows = rows_of(s, wide)
            value = back * src[at(d), rows, :] - step0_row * two[at(d), rows, :]
            return carry + value * value

        return over(step, total)

    total_res = zero
    for d in range(REACH - 1, planes):
        total_res = square_res(d, total_res)
    for k in range(1, REACH - 1):
        arrive(1, [k], two)
        total_res = square_res(REACH - 1 - k, total_res)
        if k < REACH - 2:
            across(two, fin, REACH - 1 - k, REACH - k)
    total_res = square_res(0, total_res)
    post(1, total_res)
    send(2, *range(REACH - 1))
    across(two, fin, 0, 2)
    along(2, two, fin)
    share(1, fin, 0)
    arrive(2, [REACH - 1, 0], fin)
    share(1, fin, 1)

    norm1, _ = collect(1)
    ratio = norm1 / norm0
    keep = 1.0 - step0 * squared + ratio
    keep_row = spread(keep)

    def square_dir(d, total):
        def step(s, carry):
            rows = rows_of(s, wide)
            value = keep_row * src[at(d), rows, :] - step0_row * two[at(d), rows, :]
            return carry + value * value

        return over(step, total)

    def square_fin(d, total):
        def step(s, carry):
            rows = rows_of(s, wide)
            value = keep_row * img[at(d), rows, :] - step0_row * fin[at(d), rows, :]
            return carry + value * value

        return over(step, total)

    def loop_over(low, high, body, total):
        return lax.fori_loop(low, high, body, total)

    total_dir = loop_over(0, planes, square_dir, zero)
    total_fin = loop_over(REACH - 1, planes, square_fin, zero)
    for k in range(1, REACH - 1):
        arrive(2, [k], fin)
        if REACH - 1 - k >= late:
            share(1, fin, k + 1)
        total_fin = square_fin(REACH - 1 - k, total_fin)
    total_fin = square_fin(0, total_fin)
    post(2, total_dir, total_fin)
    form_dir, form_fin = collect(2)
    step1 = norm1 / (form_fin + squared * form_dir)

    near_img = -4.0 * (step0 + step1 * keep)
    near_fin = 4.0 * (step1 * step0)
    mix[3, 0] = jnp.broadcast_to(near_img, mix.shape[2:])
    mix[3, 1] = jnp.broadcast_to(near_fin, mix.shape[2:])

    def tell(slot):
        return pltpu.make_async_remote_copy(
            src_ref=mix.at[3], dst_ref=mix.at[slot],
            send_sem=mix_s.at[slot], recv_sem=mix_r.at[slot],
            device_id={"orb": quarters[slot]}, device_id_type=pl.DeviceIdType.MESH)

    near_img_row = spread(near_img)
    near_fin_row = spread(near_fin)

    def respond(slot, d):
        rows = rows_in(slot)
        return orb[at(d), rows, :] * (
            near_img_row * img[at(d), rows, :] + near_fin_row * fin[at(d), rows, :])

    def late_copy(slot):
        return pltpu.make_async_remote_copy(
            src_ref=ship_late.at[slot], dst_ref=land_late.at[slot],
            send_sem=late_s.at[slot], recv_sem=late_r.at[slot],
            device_id={"orb": quarters[slot]}, device_id_type=pl.DeviceIdType.MESH)

    for slot in range(3):
        for d in range(late):
            ship_late[slot, d] = respond(slot, d)
        tell(slot).start()
        late_copy(slot).start()

    @pl.when(has_slow)
    def _():
        slow_sent(0).wait_send()

    fast(0).wait_send()
    sol_src = spread(step0 + step1 * keep)
    sol_two = spread(step1 * step0)

    def solve(p, carry):
        def step(s, inner):
            rows = rows_of(s, wide)
            src[p, rows, :] = sol_src * src[p, rows, :] - sol_two * two[p, rows, :]
            return inner

        return over(step, carry)

    lax.fori_loop(0, planes, solve, 0)
    for d in range(planes):
        dens[at(d)] = respond(3, d)
    for slot in range(3):
        tell(slot).wait_recv()
    for batch, (d, count) in enumerate(batches[0]):
        for slot in range(3):
            ship_copy(0, slot, d, count, batch).wait_recv()
    for batch, (d, count) in enumerate(batches[1]):
        for slot in range(3):
            ship_copy(1, slot, d, count, batch).wait_recv()
        for e in range(d, d + count):
            total = dens[at(e)]
            for slot in range(3):
                for field in range(2):
                    total = total + mix[slot, field, 0:1, :] * land[field, slot, e - late]
            dens[at(e)] = total
    for slot in range(3):
        late_copy(slot).wait_recv()
    for d in range(late):
        dens[at(d)] = dens[at(d)] + (land_late[0, d] + land_late[1, d] + land_late[2, d])

    @pl.when(has_slow)
    def _():
        slow_sent(1).wait_send()
        slow_sent(2).wait_send()

    fast(1).wait_send()
    fast(2).wait_send()
    for r in range(3):
        exchanged(r).wait_send()
    pltpu.make_async_remote_copy(
        src_ref=ship, dst_ref=land, send_sem=ship_s, recv_sem=ship_r.at[0, 0, 0],
        device_id={"orb": both}, device_id_type=pl.DeviceIdType.MESH).wait_send()
    for slot in range(3):
        tell(slot).wait_send()
        late_copy(slot).wait_send()


def write_out(sol, den, sol_hbm, den_hbm, sem):
    copies = [
        pltpu.make_async_copy(sol, sol_hbm, sem.at[0]),
        pltpu.make_async_copy(den, den_hbm, sem.at[1]),
    ]
    for copy in copies:
        copy.start()
    for copy in copies:
        copy.wait()


def body(n, groups, orbitals, potential, trial_potential, eigenvalues, frequency):
    count, planes, ny, nz = orbitals.shape
    assert count == 1 and groups == 4 and n % 2 == 0
    assert planes >= 2 * REACH and planes // 4 < REACH
    assert ny % 32 == 0 and nz % 128 == 0 and min(ny, nz) > 2 * REACH
    quarter = ny // groups
    late = planes // 4
    early = planes - late
    f32 = jnp.float32
    field = pltpu.VMEM((planes, ny, nz), f32)
    dma = pltpu.SemaphoreType.DMA
    anywhere = pl.BlockSpec(memory_space=pl.ANY)
    hbm = pl.BlockSpec(memory_space=pltpu.HBM)
    vmem = pl.BlockSpec(memory_space=pltpu.VMEM)
    sol, den = pl.pallas_call(
        functools.partial(kernel, n),
        out_shape=(
            pltpu.VMEM((planes, ny, nz), f32),
            pltpu.VMEM((planes, quarter, nz), f32),
        ),
        in_specs=[hbm] * 5,
        out_specs=(vmem, vmem),
        scratch_shapes=[field] * 6 + [
            pltpu.VMEM((2, nz, nz), jnp.bfloat16),
            pltpu.VMEM((2, ny, ny), jnp.bfloat16),
            pltpu.VMEM((3, REACH, ny, nz), f32),
            pltpu.VMEM((3, REACH, ny, nz), f32),
            pltpu.VMEM((3, n, 2, 128), f32),
            pltpu.VMEM((2, 3, early, quarter, nz), f32),
            pltpu.VMEM((2, 3, early, quarter, nz), f32),
            pltpu.VMEM((3, late, quarter, nz), f32),
            pltpu.VMEM((3, late, quarter, nz), f32),
            pltpu.VMEM((4, 2, 8, nz), f32),
            pltpu.SMEM((1,), f32), pltpu.SMEM((1,), f32),
            dma((2, planes)), dma((3,)),
            dma((3,)), dma((3, REACH)), dma((3,)), dma((3,)), dma((3,)), dma((3,)),
            dma(()), dma((2, 3, 1 + REACH)), dma((3,)), dma((3,)), dma((3,)), dma((3,)),
        ],
        compiler_params=pltpu.CompilerParams(
            collective_id=0, has_side_effects=True, vmem_limit_bytes=50 * 2**20),
        name="sternheimer",
    )(
        orbitals.reshape(planes, ny, nz), potential, trial_potential,
        eigenvalues, frequency,
    )
    sol, den = pl.pallas_call(
        write_out,
        out_shape=(jax.ShapeDtypeStruct(sol.shape, f32), jax.ShapeDtypeStruct(den.shape, f32)),
        in_specs=[vmem] * 2,
        out_specs=(anywhere, anywhere),
        scratch_shapes=[dma((2,))],
        compiler_params=pltpu.CompilerParams(vmem_limit_bytes=2**20),
        name="write_out",
    )(sol, den)
    return sol.reshape(orbitals.shape), den


def solution(mesh):
    in_specs = (
        P("orb", "grid", None, None),
        P("grid", None, None),
        P("grid", None, None),
        P("orb"),
        P(),
    )
    out_specs = (P("orb", "grid", None, None), P("grid", "orb", None))
    call = functools.partial(body, mesh.shape["grid"], mesh.shape["orb"])
    return jax.shard_map(call, mesh=mesh, in_specs=in_specs, out_specs=out_specs, check_vma=False)
```

```python
import functools

import jax
import jax.numpy as jnp
from jax import lax
from jax.experimental import pallas as pl
from jax.experimental.pallas import tpu as pltpu
from jax.sharding import PartitionSpec as P

STENCIL = (
    -5369.0 / 1800.0,
    12.0 / 7.0,
    -15.0 / 56.0,
    10.0 / 189.0,
    -1.0 / 112.0,
    2.0 / 1925.0,
    -1.0 / 16632.0,
)
SPACING = 0.75
REACH = len(STENCIL) - 1
COEFS = tuple(-0.5 / (SPACING * SPACING) * c for c in STENCIL)
STRIP = 8


def circulant(ref, count):
    size = ref.shape[1]

    def step(s, carry):
        rows = pl.ds(pl.multiple_of(s * count, count), count)
        row = s * count + lax.broadcasted_iota(jnp.int32, (count, size), 0)
        apart = jnp.abs(row - lax.broadcasted_iota(jnp.int32, (count, size), 1))
        apart = jnp.minimum(apart, size - apart)
        full = jnp.zeros((count, size), jnp.float32)
        for k in range(1, REACH + 1):
            full = jnp.where(apart == k, COEFS[k], full)
        high = full.astype(jnp.bfloat16)
        ref[0, rows, :] = high
        ref[1, rows, :] = (full - high.astype(jnp.float32)).astype(jnp.bfloat16)
        return carry

    lax.fori_loop(0, size // count, step, 0)


def kernel(
    n,
    orb_hbm, pot_hbm, tri_hbm, eig_hbm, freq_hbm,
    src, dens,
    orb, pot, tri, img, two, fin, cz, cy,
    hslow, hfast, sums, ship, land, ship_late, land_late, mix,
    eig, freq, met, ld_sem, mat_sem,
    slow_s, slow_r, fast_s, fast_r, sum_s, sum_r,
    ship_s, ship_r, late_s, late_r, mix_s, mix_r,
):
    planes, ny, nz = src.shape
    wide = 32
    late = ship_late.shape[1]
    quarter = ship.shape[3]
    g = lax.axis_index("grid")
    o = lax.axis_index("orb")
    odd = lax.rem(g, 2)
    slow_id = lax.rem(g + n - 1 + 2 * odd, n)
    fast_id = g + 1 - 2 * odd
    has_slow = jnp.logical_and(g + odd > 0, g + odd < n)
    flip1 = o + 1 - 2 * lax.rem(o, 2)
    flip2 = lax.rem(o + 2, 4)
    first = (1 - odd) * flip1 + odd * flip2
    second = odd * flip1 + (1 - odd) * flip2
    both = 3 - o
    quarters = (both, first, second, o)

    barrier = pltpu.get_barrier_semaphore()
    @pl.when(has_slow)
    def _():
        pl.semaphore_signal(barrier, inc=1, device_id={"grid": slow_id})

    pl.semaphore_signal(barrier, inc=1, device_id={"grid": fast_id})
    for slot in range(3):
        pl.semaphore_signal(barrier, inc=1, device_id={"orb": quarters[slot]})

    def at(d):
        return d + odd * (planes - 1 - 2 * d)

    def span(d, count):
        return pl.ds(d + odd * (planes - count - 2 * d), count)

    def meet(i):
        reach = 2 ** i
        for peer in (g - reach, g + reach):
            @pl.when(jnp.logical_and(peer >= 0, peer < n))
            def _():
                pl.semaphore_signal(met.at[i], inc=1, device_id={"grid": peer})

    def met_by(i):
        reach = 2 ** i
        pl.semaphore_wait(
            met.at[i], jnp.where(g >= reach, 1, 0) + jnp.where(g + reach < n, 1, 0))

    rounds = met.shape[0]

    def load(which, d):
        hbm, ref = ((orb_hbm, orb), (tri_hbm, tri))[which]
        return pltpu.make_async_copy(hbm.at[at(d)], ref.at[at(d)], ld_sem.at[which, d])

    order = list(range(REACH)) + list(range(planes - 1, REACH - 1, -1))
    for d in order:
        load(0, d).start()
        load(1, d).start()
    mats = [
        pltpu.make_async_copy(pot_hbm, pot, mat_sem.at[0]),
        pltpu.make_async_copy(eig_hbm, eig, mat_sem.at[1]),
        pltpu.make_async_copy(freq_hbm, freq, mat_sem.at[2]),
    ]
    for copy in mats:
        copy.start()

    fields = (src, img, two)

    def slow(r, k):
        return pltpu.make_async_remote_copy(
            src_ref=fields[r].at[at(k)], dst_ref=hslow.at[r, k],
            send_sem=slow_s.at[r], recv_sem=slow_r.at[r, k],
            device_id={"grid": slow_id}, device_id_type=pl.DeviceIdType.MESH)

    def slow_sent(r):
        return pltpu.make_async_remote_copy(
            src_ref=fields[r].at[span(0, REACH)], dst_ref=hslow.at[r],
            send_sem=slow_s.at[r], recv_sem=slow_r.at[r, 0],
            device_id={"grid": slow_id}, device_id_type=pl.DeviceIdType.MESH)

    def fast(r):
        return pltpu.make_async_remote_copy(
            src_ref=fields[r].at[span(planes - REACH, REACH)], dst_ref=hfast.at[r],
            send_sem=fast_s.at[r], recv_sem=fast_r.at[r],
            device_id={"grid": fast_id}, device_id_type=pl.DeviceIdType.MESH)

    def send(r, *ks):
        @pl.when(has_slow)
        def _():
            for k in ks:
                slow(r, k).start()

    def rows_in(slot):
        return pl.ds(pl.multiple_of(quarters[slot] * quarter, 8), quarter)

    def rows_of(s, count):
        return pl.ds(pl.multiple_of(s * count, count), count)

    def over(step, init, count=wide):
        return lax.fori_loop(0, ny // count, step, init)

    def ship_copy(field, slot, d, count, sem):
        piece = pl.ds(d - late, count)
        return pltpu.make_async_remote_copy(
            src_ref=ship.at[field, slot, piece], dst_ref=land.at[field, slot, piece],
            send_sem=ship_s, recv_sem=ship_r.at[field, slot, sem],
            device_id={"orb": quarters[slot]}, device_id_type=pl.DeviceIdType.MESH)

    cut = REACH + late
    lead = [REACH - 1, REACH - 2]
    rest = list(range(REACH - 2))
    batches = (
        ((REACH, planes - REACH), (late, REACH - late)),
        ((cut, planes - cut), (REACH, cut - REACH)) + tuple((d, 1) for d in range(REACH - 1, late - 1, -1)),
    )

    def share(field, value, batch):
        d, count = batches[field][batch]
        for slot in range(3):
            rows = rows_in(slot)
            for e in range(d, d + count):
                ship[field, slot, e - late] = orb[at(e), rows, :] * value[at(e), rows, :]
            ship_copy(field, slot, d, count, batch).start()

    zero = jnp.zeros((wide, nz), jnp.float32)

    def arrive(r, ks, acc):
        @pl.when(has_slow)
        def _():
            for k in ks:
                slow(r, k).wait_recv()

            def step(s, carry):
                rows = rows_of(s, wide)
                values = [hslow[r, k, rows, :] for k in ks]
                for d in range(REACH):
                    terms = [COEFS[d + 1 + k] * v for k, v in zip(ks, values) if d + k < REACH]
                    if terms:
                        acc[at(d), rows, :] = acc[at(d), rows, :] + functools.reduce(jnp.add, terms)
                return carry

            over(step, 0)

    def square_of(ref, d, total):
        def step(s, carry):
            value = ref[at(d), rows_of(s, wide), :]
            return carry + value * value

        return over(step, total)

    def across(value, out, low, high):
        def plane(d):
            p = at(d)
            whole = value[p]
            high_part = whole.astype(jnp.bfloat16)
            low_part = (whole - high_part.astype(jnp.float32)).astype(jnp.bfloat16)
            product = functools.partial(jnp.dot, preferred_element_type=jnp.float32)
            along_z = product(high_part, cz[0]) + product(low_part, cz[0]) + product(high_part, cz[1])
            along_y = product(cy[0], high_part) + product(cy[0], low_part) + product(cy[1], high_part)
            out[p] = along_z + along_y

        count = high - low
        size = max(k for k in range(1, REACH + 1) if count % k == 0)

        def group(i, carry):
            for j in range(size):
                plane(low + i * size + j)
            return carry

        lax.fori_loop(0, count // size, group, 0)

    def along(r, value, out, low, high):
        for side in (0, 1):
            @pl.when(odd == side)
            def _(side=side):
                def place(d):
                    return planes - 1 - d if side else d

                def part(d, rows):
                    if d < planes:
                        return value[place(d), rows, :]
                    k = d - planes
                    return hfast[r, REACH - 1 - k if side else k, rows, :]

                def strip(s, carry):
                    rows = rows_of(s, STRIP)
                    parts = {
                        d: part(d, rows)
                        for d in range(max(0, low - REACH), min(planes, high) + REACH)
                        if d < high + REACH
                    }
                    for d in range(low, high):
                        here = out.at[place(d), rows, :]
                        total = here[...] + (pot[place(d), rows, :] + (3.0 * COEFS[0] - energy)) * parts[d]
                        for k in range(1, REACH + 1):
                            near = [parts[e] for e in (d - k, d + k) if e in parts]
                            total = total + COEFS[k] * (near[0] + near[1] if len(near) == 2 else near[0])
                        here[...] = total
                    return carry

                over(strip, 0, STRIP)

    def fold(total):
        total = functools.reduce(
            lambda a, b: a + b, [total[i:i + 8] for i in range(0, wide, 8)])
        total = functools.reduce(
            lambda a, b: a + b, [total[:, i:i + 128] for i in range(0, nz, 128)])
        return jnp.sum(total, axis=0, keepdims=True)

    def exchange(r, j, slot):
        return pltpu.make_async_remote_copy(
            src_ref=sums.at[r, slot], dst_ref=sums.at[r, slot],
            send_sem=sum_s.at[r], recv_sem=sum_r.at[r],
            device_id={"grid": lax.rem(g + j, n)}, device_id_type=pl.DeviceIdType.MESH)

    def exchanged(r):
        return pltpu.make_async_remote_copy(
            src_ref=sums.at[r, pl.ds(0, n - 1)], dst_ref=sums.at[r, pl.ds(0, n - 1)],
            send_sem=sum_s.at[r], recv_sem=sum_r.at[r],
            device_id={"grid": fast_id}, device_id_type=pl.DeviceIdType.MESH)

    def post(r, *totals):
        for i in range(2):
            row = fold(totals[i]) if i < len(totals) else jnp.zeros((1, 128), jnp.float32)
            sums[r, g, i:i + 1, :] = row
        for j in range(1, n):
            exchange(r, j, g).start()

    def collect(r):
        exchanged(r).wait_recv()
        total = sums[r, 0]
        for m in range(1, n):
            total = total + sums[r, m]
        return tuple(jnp.sum(total[i:i + 1], keepdims=True) for i in range(2))

    def spread(value):
        return jnp.broadcast_to(value, (1, nz))

    circulant(cz, 32)
    circulant(cy, 32)

    total_src = zero
    for d in order:
        load(0, d).wait()
        load(1, d).wait()

        def step(s, carry, d=d):
            rows = rows_of(s, wide)
            value = orb[at(d), rows, :] * tri[at(d), rows, :]
            src[at(d), rows, :] = value
            return carry + value * value

        total_src = over(step, total_src)
        if d == order[0]:
            pl.semaphore_wait(barrier, 4 + has_slow.astype(jnp.int32))
            meet(0)
        if d < REACH:
            send(0, d)
    fast(0).start()
    for copy in mats:
        copy.wait()
    energy = eig[0]
    squared = freq[0] * freq[0]

    across(src, img, REACH, planes)
    if rounds > 1:
        met_by(0)
        meet(1)
    fast(0).wait_recv()
    along(0, src, img, REACH, planes)
    fast(1).start()
    share(0, img, 0)
    across(src, img, 0, REACH)
    along(0, src, img, 0, REACH)
    for i in range(1, rounds - 1):
        met_by(i)
        meet(i + 1)
    total_img = zero
    for d in range(REACH, planes):
        total_img = square_of(img, d, total_img)
    early = list(range(REACH - late))
    arrive(0, early, img)
    send(1, *lead)
    share(0, img, 1)
    for k in early:
        total_img = square_of(img, REACH - 1 - k, total_img)
    across(img, two, late, planes)
    for k in range(REACH - late, REACH):
        arrive(0, [k], img)
        total_img = square_of(img, REACH - 1 - k, total_img)
        if k < REACH - 1:
            across(img, two, REACH - 1 - k, REACH - k)
    met_by(rounds - 1)
    post(0, total_src, total_img)
    send(1, *rest)
    across(img, two, 0, 1)
    fast(1).wait_recv()
    along(1, img, two, 0, planes)
    fast(2).start()

    across(two, fin, REACH, planes)
    arrive(1, [*lead, 0], two)
    send(2, REACH - 1)
    across(two, fin, REACH - 1, REACH)
    norm0, form0 = collect(0)
    step0 = norm0 / (form0 + squared * norm0)
    back = spread(1.0 - step0 * squared)
    step0_row = spread(step0)

    def square_res(d, total):
        def step(s, carry):
            rows = rows_of(s, wide)
            value = back * src[at(d), rows, :] - step0_row * two[at(d), rows, :]
            return carry + value * value

        return over(step, total)

    total_res = zero
    for d in range(REACH - 1, planes):
        total_res = square_res(d, total_res)
    for k in range(1, REACH - late):
        arrive(1, [k], two)
        d = REACH - 1 - k
        if d in lead:
            send(2, d)
        total_res = square_res(d, total_res)
        across(two, fin, d, d + 1)
    fast(2).wait_recv()
    along(2, two, fin, cut, planes)
    share(1, fin, 0)
    for k in range(REACH - late, rest[-1] + 1):
        arrive(1, [k], two)
    for d in range(late):
        total_res = square_res(d, total_res)
    post(1, total_res)
    send(2, *rest)
    across(two, fin, 0, late)
    along(2, two, fin, 0, cut)
    share(1, fin, 1)
    arrive(2, [*lead, 0], fin)
    share(1, fin, 2)

    norm1, _ = collect(1)
    ratio = norm1 / norm0
    keep = 1.0 - step0 * squared + ratio
    keep_row = spread(keep)

    def square_dir(d, total):
        def step(s, carry):
            rows = rows_of(s, wide)
            value = keep_row * src[at(d), rows, :] - step0_row * two[at(d), rows, :]
            return carry + value * value

        return over(step, total)

    def square_fin(d, total):
        def step(s, carry):
            rows = rows_of(s, wide)
            value = keep_row * img[at(d), rows, :] - step0_row * fin[at(d), rows, :]
            return carry + value * value

        return over(step, total)

    def loop_over(low, high, body, total):
        return lax.fori_loop(low, high, body, total)

    total_dir = loop_over(0, planes, square_dir, zero)
    total_fin = loop_over(REACH - 1, planes, square_fin, zero)
    for k in rest[1:]:
        arrive(2, [k], fin)
        if REACH - 1 - k >= late:
            share(1, fin, k + 2)
            total_fin = square_fin(REACH - 1 - k, total_fin)
    for d in range(late):
        total_fin = square_fin(d, total_fin)
    post(2, total_dir, total_fin)
    form_dir, form_fin = collect(2)
    step1 = norm1 / (form_fin + squared * form_dir)

    near_img = -4.0 * (step0 + step1 * keep)
    near_fin = 4.0 * (step1 * step0)
    mix[3, 0] = jnp.broadcast_to(near_img, mix.shape[2:])
    mix[3, 1] = jnp.broadcast_to(near_fin, mix.shape[2:])

    def tell(slot):
        return pltpu.make_async_remote_copy(
            src_ref=mix.at[3], dst_ref=mix.at[slot],
            send_sem=mix_s.at[slot], recv_sem=mix_r.at[slot],
            device_id={"orb": quarters[slot]}, device_id_type=pl.DeviceIdType.MESH)

    near_img_row = spread(near_img)
    near_fin_row = spread(near_fin)

    def respond(slot, d):
        rows = rows_in(slot)
        return orb[at(d), rows, :] * (
            near_img_row * img[at(d), rows, :] + near_fin_row * fin[at(d), rows, :])

    def late_copy(slot):
        return pltpu.make_async_remote_copy(
            src_ref=ship_late.at[slot], dst_ref=land_late.at[slot],
            send_sem=late_s.at[slot], recv_sem=late_r.at[slot],
            device_id={"orb": quarters[slot]}, device_id_type=pl.DeviceIdType.MESH)

    for slot in range(3):
        for d in range(late):
            ship_late[slot, d] = respond(slot, d)
        tell(slot).start()
        late_copy(slot).start()

    @pl.when(has_slow)
    def _():
        slow_sent(0).wait_send()

    fast(0).wait_send()
    sol_src = spread(step0 + step1 * keep)
    sol_two = spread(step1 * step0)

    def solve(p, carry):
        def step(s, inner):
            rows = rows_of(s, wide)
            src[p, rows, :] = sol_src * src[p, rows, :] - sol_two * two[p, rows, :]
            return inner

        return over(step, carry)

    lax.fori_loop(0, planes, solve, 0)
    for d in range(planes):
        dens[at(d)] = respond(3, d)
    for slot in range(3):
        tell(slot).wait_recv()
    for batch, (d, count) in enumerate(batches[0]):
        for slot in range(3):
            ship_copy(0, slot, d, count, batch).wait_recv()
    for batch, (d, count) in enumerate(batches[1]):
        for slot in range(3):
            ship_copy(1, slot, d, count, batch).wait_recv()
        for e in range(d, d + count):
            total = dens[at(e)]
            for slot in range(3):
                for field in range(2):
                    total = total + mix[slot, field, 0:1, :] * land[field, slot, e - late]
            dens[at(e)] = total
    for slot in range(3):
        late_copy(slot).wait_recv()
    for d in range(late):
        dens[at(d)] = dens[at(d)] + (land_late[0, d] + land_late[1, d] + land_late[2, d])

    @pl.when(has_slow)
    def _():
        slow_sent(1).wait_send()
        slow_sent(2).wait_send()

    fast(1).wait_send()
    fast(2).wait_send()
    for r in range(3):
        exchanged(r).wait_send()
    pltpu.make_async_remote_copy(
        src_ref=ship, dst_ref=land, send_sem=ship_s, recv_sem=ship_r.at[0, 0, 0],
        device_id={"orb": both}, device_id_type=pl.DeviceIdType.MESH).wait_send()
    for slot in range(3):
        tell(slot).wait_send()
        late_copy(slot).wait_send()


def write_out(sol, den, sol_hbm, den_hbm, sem):
    copies = [
        pltpu.make_async_copy(sol, sol_hbm, sem.at[0]),
        pltpu.make_async_copy(den, den_hbm, sem.at[1]),
    ]
    for copy in copies:
        copy.start()
    for copy in copies:
        copy.wait()


def body(n, groups, orbitals, potential, trial_potential, eigenvalues, frequency):
    count, planes, ny, nz = orbitals.shape
    assert count == 1 and groups == 4 and n % 2 == 0
    assert planes >= 2 * REACH
    assert ny % 32 == 0 and nz % 128 == 0 and min(ny, nz) > 2 * REACH
    quarter = ny // groups
    late = REACH // 2
    early = planes - late
    f32 = jnp.float32
    field = pltpu.VMEM((planes, ny, nz), f32)
    dma = pltpu.SemaphoreType.DMA
    anywhere = pl.BlockSpec(memory_space=pl.ANY)
    hbm = pl.BlockSpec(memory_space=pltpu.HBM)
    vmem = pl.BlockSpec(memory_space=pltpu.VMEM)
    sol, den = pl.pallas_call(
        functools.partial(kernel, n),
        out_shape=(
            pltpu.VMEM((planes, ny, nz), f32),
            pltpu.VMEM((planes, quarter, nz), f32),
        ),
        in_specs=[hbm] * 5,
        out_specs=(vmem, vmem),
        scratch_shapes=[field] * 6 + [
            pltpu.VMEM((2, nz, nz), jnp.bfloat16),
            pltpu.VMEM((2, ny, ny), jnp.bfloat16),
            pltpu.VMEM((3, REACH, ny, nz), f32),
            pltpu.VMEM((3, REACH, ny, nz), f32),
            pltpu.VMEM((3, n, 2, 128), f32),
            pltpu.VMEM((2, 3, early, quarter, nz), f32),
            pltpu.VMEM((2, 3, early, quarter, nz), f32),
            pltpu.VMEM((3, late, quarter, nz), f32),
            pltpu.VMEM((3, late, quarter, nz), f32),
            pltpu.VMEM((4, 2, 8, nz), f32),
            pltpu.SMEM((1,), f32), pltpu.SMEM((1,), f32),
            pltpu.SemaphoreType.REGULAR(((n - 1).bit_length(),)),
            dma((2, planes)), dma((3,)),
            dma((3,)), dma((3, REACH)), dma((3,)), dma((3,)), dma((3,)), dma((3,)),
            dma(()), dma((2, 3, 2 + REACH)), dma((3,)), dma((3,)), dma((3,)), dma((3,)),
        ],
        compiler_params=pltpu.CompilerParams(
            collective_id=0, has_side_effects=True, vmem_limit_bytes=50 * 2**20),
        name="sternheimer",
    )(
        orbitals.reshape(planes, ny, nz), potential, trial_potential,
        eigenvalues, frequency,
    )
    sol, den = pl.pallas_call(
        write_out,
        out_shape=(jax.ShapeDtypeStruct(sol.shape, f32), jax.ShapeDtypeStruct(den.shape, f32)),
        in_specs=[vmem] * 2,
        out_specs=(anywhere, anywhere),
        scratch_shapes=[dma((2,))],
        compiler_params=pltpu.CompilerParams(vmem_limit_bytes=2**20),
        name="write_out",
    )(sol, den)
    return sol.reshape(orbitals.shape), den


def solution(mesh):
    in_specs = (
        P("orb", "grid", None, None),
        P("grid", None, None),
        P("grid", None, None),
        P("orb"),
        P(),
    )
    out_specs = (P("orb", "grid", None, None), P("grid", "orb", None))
    call = functools.partial(body, mesh.shape["grid"], mesh.shape["orb"])
    return jax.shard_map(call, mesh=mesh, in_specs=in_specs, out_specs=out_specs, check_vma=False)
```

```python
import functools

import jax
import jax.numpy as jnp
from jax import lax
from jax.experimental import pallas as pl
from jax.experimental.pallas import tpu as pltpu
from jax.sharding import PartitionSpec as P

STENCIL = (
    -5369.0 / 1800.0,
    12.0 / 7.0,
    -15.0 / 56.0,
    10.0 / 189.0,
    -1.0 / 112.0,
    2.0 / 1925.0,
    -1.0 / 16632.0,
)
SPACING = 0.75
REACH = len(STENCIL) - 1
COEFS = tuple(-0.5 / (SPACING * SPACING) * c for c in STENCIL)
STRIP = 8


def circulant(ref, count):
    size = ref.shape[1]

    def step(s, carry):
        rows = pl.ds(pl.multiple_of(s * count, count), count)
        row = s * count + lax.broadcasted_iota(jnp.int32, (count, size), 0)
        apart = jnp.abs(row - lax.broadcasted_iota(jnp.int32, (count, size), 1))
        apart = jnp.minimum(apart, size - apart)
        full = jnp.zeros((count, size), jnp.float32)
        for k in range(1, REACH + 1):
            full = jnp.where(apart == k, COEFS[k], full)
        high = full.astype(jnp.bfloat16)
        ref[0, rows, :] = high
        ref[1, rows, :] = (full - high.astype(jnp.float32)).astype(jnp.bfloat16)
        return carry

    lax.fori_loop(0, size // count, step, 0)


def kernel(
    n,
    orb_hbm, pot_hbm, tri_hbm, eig_hbm, freq_hbm,
    src, dens,
    orb, pot, tri, img, two, fin, cz, cy,
    hslow, hfast, sums, ship, land, ship_late, land_late, mix,
    eig, freq, met, ld_sem, mat_sem,
    slow_s, slow_r, fast_s, fast_r, sum_s, sum_r,
    ship_s, ship_r, late_s, late_r, mix_s, mix_r,
):
    planes, ny, nz = src.shape
    wide = 32
    late = ship_late.shape[1]
    quarter = ship.shape[3]
    g = lax.axis_index("grid")
    o = lax.axis_index("orb")
    odd = lax.rem(g, 2)
    slow_id = lax.rem(g + n - 1 + 2 * odd, n)
    fast_id = g + 1 - 2 * odd
    has_slow = jnp.logical_and(g + odd > 0, g + odd < n)
    flip1 = o + 1 - 2 * lax.rem(o, 2)
    flip2 = lax.rem(o + 2, 4)
    first = (1 - odd) * flip1 + odd * flip2
    second = odd * flip1 + (1 - odd) * flip2
    both = 3 - o
    quarters = (both, first, second, o)

    barrier = pltpu.get_barrier_semaphore()
    @pl.when(has_slow)
    def _():
        pl.semaphore_signal(barrier, inc=1, device_id={"grid": slow_id})

    pl.semaphore_signal(barrier, inc=1, device_id={"grid": fast_id})
    for slot in range(3):
        pl.semaphore_signal(barrier, inc=1, device_id={"orb": quarters[slot]})

    def at(d):
        return d + odd * (planes - 1 - 2 * d)

    def span(d, count):
        return pl.ds(d + odd * (planes - count - 2 * d), count)

    def meet(i):
        reach = 2 ** i
        for peer in (g - reach, g + reach):
            @pl.when(jnp.logical_and(peer >= 0, peer < n))
            def _():
                pl.semaphore_signal(met.at[i], inc=1, device_id={"grid": peer})

    def met_by(i):
        reach = 2 ** i
        pl.semaphore_wait(
            met.at[i], jnp.where(g >= reach, 1, 0) + jnp.where(g + reach < n, 1, 0))

    rounds = met.shape[0]

    def load(which, d):
        hbm, ref = ((orb_hbm, orb), (tri_hbm, tri))[which]
        return pltpu.make_async_copy(hbm.at[at(d)], ref.at[at(d)], ld_sem.at[which, d])

    order = list(range(REACH)) + list(range(planes - 1, REACH - 1, -1))
    for d in order:
        load(0, d).start()
        load(1, d).start()
    mats = [
        pltpu.make_async_copy(pot_hbm, pot, mat_sem.at[0]),
        pltpu.make_async_copy(eig_hbm, eig, mat_sem.at[1]),
        pltpu.make_async_copy(freq_hbm, freq, mat_sem.at[2]),
    ]
    for copy in mats:
        copy.start()

    fields = (src, img, two)

    def slow(r, k):
        return pltpu.make_async_remote_copy(
            src_ref=fields[r].at[at(k)], dst_ref=hslow.at[r, k],
            send_sem=slow_s.at[r], recv_sem=slow_r.at[r, k],
            device_id={"grid": slow_id}, device_id_type=pl.DeviceIdType.MESH)

    def slow_sent(r):
        return pltpu.make_async_remote_copy(
            src_ref=fields[r].at[span(0, REACH)], dst_ref=hslow.at[r],
            send_sem=slow_s.at[r], recv_sem=slow_r.at[r, 0],
            device_id={"grid": slow_id}, device_id_type=pl.DeviceIdType.MESH)

    half = REACH // 2

    def fast(r, i):
        return pltpu.make_async_remote_copy(
            src_ref=fields[r].at[span(planes - half * (i + 1), half)],
            dst_ref=hfast.at[r, pl.ds(half * (1 - i) + odd * half * (2 * i - 1), half)],
            send_sem=fast_s.at[r], recv_sem=fast_r.at[r, i],
            device_id={"grid": fast_id}, device_id_type=pl.DeviceIdType.MESH)

    def fast_send(r):
        fast(r, 0).start()
        fast(r, 1).start()

    def fast_wait(r):
        fast(r, 0).wait_recv()
        fast(r, 1).wait_recv()

    def fast_sent(r):
        pltpu.make_async_remote_copy(
            src_ref=fields[r].at[span(planes - REACH, REACH)], dst_ref=hfast.at[r],
            send_sem=fast_s.at[r], recv_sem=fast_r.at[r, 0],
            device_id={"grid": fast_id}, device_id_type=pl.DeviceIdType.MESH).wait_send()

    def send(r, *ks):
        @pl.when(has_slow)
        def _():
            for k in ks:
                slow(r, k).start()

    def rows_in(slot):
        return pl.ds(pl.multiple_of(quarters[slot] * quarter, 8), quarter)

    def rows_of(s, count):
        return pl.ds(pl.multiple_of(s * count, count), count)

    def over(step, init, count=wide):
        return lax.fori_loop(0, ny // count, step, init)

    def ship_copy(field, slot, d, count, sem):
        piece = pl.ds(d - late, count)
        return pltpu.make_async_remote_copy(
            src_ref=ship.at[field, slot, piece], dst_ref=land.at[field, slot, piece],
            send_sem=ship_s, recv_sem=ship_r.at[field, slot, sem],
            device_id={"orb": quarters[slot]}, device_id_type=pl.DeviceIdType.MESH)

    cut = 2 * REACH - half
    lead = [REACH - 1, REACH - 2]
    rest = list(range(REACH - 2))
    batches = (
        ((REACH, planes - REACH), (late, REACH - late)),
        ((2 * REACH - 1, planes - 2 * REACH + 1),)
        + tuple((d, 1) for d in range(2 * REACH - 2, cut - 1, -1))
        + ((REACH, cut - REACH),)
        + tuple((d, 1) for d in range(REACH - 1, late - 1, -1)),
    )

    def share(field, value, batch):
        d, count = batches[field][batch]
        for slot in range(3):
            rows = rows_in(slot)
            for e in range(d, d + count):
                ship[field, slot, e - late] = orb[at(e), rows, :] * value[at(e), rows, :]
            ship_copy(field, slot, d, count, batch).start()

    zero = jnp.zeros((wide, nz), jnp.float32)

    def arrive(r, ks, acc):
        @pl.when(has_slow)
        def _():
            for k in ks:
                slow(r, k).wait_recv()

            def step(s, carry):
                rows = rows_of(s, wide)
                values = [hslow[r, k, rows, :] for k in ks]
                for d in range(REACH):
                    terms = [COEFS[d + 1 + k] * v for k, v in zip(ks, values) if d + k < REACH]
                    if terms:
                        acc[at(d), rows, :] = acc[at(d), rows, :] + functools.reduce(jnp.add, terms)
                return carry

            over(step, 0)

    def square_of(ref, d, total):
        def step(s, carry):
            value = ref[at(d), rows_of(s, wide), :]
            return carry + value * value

        return over(step, total)

    def across(value, out, low, high):
        def plane(d):
            p = at(d)
            whole = value[p]
            high_part = whole.astype(jnp.bfloat16)
            low_part = (whole - high_part.astype(jnp.float32)).astype(jnp.bfloat16)
            product = functools.partial(jnp.dot, preferred_element_type=jnp.float32)
            along_z = product(high_part, cz[0]) + product(low_part, cz[0]) + product(high_part, cz[1])
            along_y = product(cy[0], high_part) + product(cy[0], low_part) + product(cy[1], high_part)
            out[p] = along_z + along_y

        count = high - low
        size = max(k for k in range(1, REACH + 1) if count % k == 0)

        def group(i, carry):
            for j in range(size):
                plane(low + i * size + j)
            return carry

        lax.fori_loop(0, count // size, group, 0)

    def along(r, value, out, low, high):
        for side in (0, 1):
            @pl.when(odd == side)
            def _(side=side):
                def place(d):
                    return planes - 1 - d if side else d

                def part(d, rows):
                    if d < planes:
                        return value[place(d), rows, :]
                    k = d - planes
                    return hfast[r, REACH - 1 - k if side else k, rows, :]

                def strip(s, carry):
                    rows = rows_of(s, STRIP)
                    parts = {
                        d: part(d, rows)
                        for d in range(max(0, low - REACH), min(planes, high) + REACH)
                        if d < high + REACH
                    }
                    for d in range(low, high):
                        here = out.at[place(d), rows, :]
                        total = here[...] + (pot[place(d), rows, :] + (3.0 * COEFS[0] - energy)) * parts[d]
                        for k in range(1, REACH + 1):
                            near = [parts[e] for e in (d - k, d + k) if e in parts]
                            total = total + COEFS[k] * (near[0] + near[1] if len(near) == 2 else near[0])
                        here[...] = total
                    return carry

                over(strip, 0, STRIP)

    def fold(total):
        total = functools.reduce(
            lambda a, b: a + b, [total[i:i + 8] for i in range(0, wide, 8)])
        total = functools.reduce(
            lambda a, b: a + b, [total[:, i:i + 128] for i in range(0, nz, 128)])
        return jnp.sum(total, axis=0, keepdims=True)

    def exchange(r, j, slot):
        return pltpu.make_async_remote_copy(
            src_ref=sums.at[r, slot], dst_ref=sums.at[r, slot],
            send_sem=sum_s.at[r], recv_sem=sum_r.at[r],
            device_id={"grid": lax.rem(g + j, n)}, device_id_type=pl.DeviceIdType.MESH)

    def exchanged(r):
        return pltpu.make_async_remote_copy(
            src_ref=sums.at[r, pl.ds(0, n - 1)], dst_ref=sums.at[r, pl.ds(0, n - 1)],
            send_sem=sum_s.at[r], recv_sem=sum_r.at[r],
            device_id={"grid": fast_id}, device_id_type=pl.DeviceIdType.MESH)

    def post(r, *totals):
        for i in range(2):
            row = fold(totals[i]) if i < len(totals) else jnp.zeros((1, 128), jnp.float32)
            sums[r, g, i:i + 1, :] = row
        for j in range(1, n):
            exchange(r, j, g).start()

    def collect(r):
        exchanged(r).wait_recv()
        total = sums[r, 0]
        for m in range(1, n):
            total = total + sums[r, m]
        return tuple(jnp.sum(total[i:i + 1], keepdims=True) for i in range(2))

    def spread(value):
        return jnp.broadcast_to(value, (1, nz))

    circulant(cz, 32)
    circulant(cy, 32)

    total_src = zero
    for d in order:
        load(0, d).wait()
        load(1, d).wait()

        def step(s, carry, d=d):
            rows = rows_of(s, wide)
            value = orb[at(d), rows, :] * tri[at(d), rows, :]
            src[at(d), rows, :] = value
            return carry + value * value

        total_src = over(step, total_src)
        if d == order[0]:
            pl.semaphore_wait(barrier, 4 + has_slow.astype(jnp.int32))
            meet(0)
        if d < REACH:
            send(0, d)
        if d == planes - half:
            fast(0, 0).start()
        if d == planes - REACH:
            fast(0, 1).start()
    for copy in mats:
        copy.wait()
    energy = eig[0]
    squared = freq[0] * freq[0]

    across(src, img, REACH, planes)
    if rounds > 1:
        met_by(0)
        meet(1)
    fast_wait(0)
    along(0, src, img, REACH, planes)
    fast_send(1)
    share(0, img, 0)
    across(src, img, 0, REACH)
    along(0, src, img, 0, REACH)
    for i in range(1, rounds - 1):
        met_by(i)
        meet(i + 1)
    total_img = zero
    for d in range(REACH, planes):
        total_img = square_of(img, d, total_img)
    early = list(range(REACH - late))
    arrive(0, early, img)
    send(1, *lead)
    share(0, img, 1)
    for k in early:
        total_img = square_of(img, REACH - 1 - k, total_img)
    across(img, two, late, planes)
    for k in range(REACH - late, REACH):
        arrive(0, [k], img)
        total_img = square_of(img, REACH - 1 - k, total_img)
        if k < REACH - 1:
            across(img, two, REACH - 1 - k, REACH - k)
    met_by(rounds - 1)
    post(0, total_src, total_img)
    send(1, *rest)
    across(img, two, 0, 1)
    fast_wait(1)
    along(1, img, two, 0, planes)
    fast_send(2)

    across(two, fin, REACH, planes)
    fast_wait(2)
    arrive(1, [*lead, 0], two)
    send(2, REACH - 1)
    across(two, fin, REACH - 1, REACH)
    along(2, two, fin, 2 * REACH - 1, planes)
    share(1, fin, 0)
    norm0, form0 = collect(0)
    step0 = norm0 / (form0 + squared * norm0)
    back = spread(1.0 - step0 * squared)
    step0_row = spread(step0)

    def square_res(d, total):
        def step(s, carry):
            rows = rows_of(s, wide)
            value = back * src[at(d), rows, :] - step0_row * two[at(d), rows, :]
            return carry + value * value

        return over(step, total)

    total_res = zero
    for d in range(REACH - 1, planes):
        total_res = square_res(d, total_res)
    for k in range(1, half):
        arrive(1, [k], two)
        d = REACH - 1 - k
        if d in lead:
            send(2, d)
        across(two, fin, d, d + 1)
        along(2, two, fin, REACH + d, REACH + d + 1)
        share(1, fin, k)
        total_res = square_res(d, total_res)
    for k in range(half, rest[-1] + 1):
        arrive(1, [k], two)
    for d in range(half):
        total_res = square_res(d, total_res)
    post(1, total_res)
    send(2, *rest)
    across(two, fin, 0, half)
    along(2, two, fin, 0, cut)
    share(1, fin, half)
    arrive(2, [*lead, 0], fin)
    share(1, fin, half + 1)

    norm1, _ = collect(1)
    ratio = norm1 / norm0
    keep = 1.0 - step0 * squared + ratio
    keep_row = spread(keep)

    def square_dir(d, total):
        def step(s, carry):
            rows = rows_of(s, wide)
            value = keep_row * src[at(d), rows, :] - step0_row * two[at(d), rows, :]
            return carry + value * value

        return over(step, total)

    def square_fin(d, total):
        def step(s, carry):
            rows = rows_of(s, wide)
            value = keep_row * img[at(d), rows, :] - step0_row * fin[at(d), rows, :]
            return carry + value * value

        return over(step, total)

    def loop_over(low, high, body, total):
        return lax.fori_loop(low, high, body, total)

    total_dir = loop_over(0, planes, square_dir, zero)
    total_fin = loop_over(REACH - 1, planes, square_fin, zero)
    for k in rest[1:]:
        arrive(2, [k], fin)
        d = REACH - 1 - k
        if k < rest[-1]:
            share(1, fin, half + 1 + k)
            total_fin = square_fin(d, total_fin)
    for d in range(REACH - rest[-1]):
        total_fin = square_fin(d, total_fin)
    post(2, total_dir, total_fin)
    for k in range(rest[-1], REACH - late):
        share(1, fin, half + 1 + k)
    form_dir, form_fin = collect(2)
    step1 = norm1 / (form_fin + squared * form_dir)

    near_img = -4.0 * (step0 + step1 * keep)
    near_fin = 4.0 * (step1 * step0)
    mix[3, 0] = jnp.broadcast_to(near_img, mix.shape[2:])
    mix[3, 1] = jnp.broadcast_to(near_fin, mix.shape[2:])

    def tell(slot):
        return pltpu.make_async_remote_copy(
            src_ref=mix.at[3], dst_ref=mix.at[slot],
            send_sem=mix_s.at[slot], recv_sem=mix_r.at[slot],
            device_id={"orb": quarters[slot]}, device_id_type=pl.DeviceIdType.MESH)

    near_img_row = spread(near_img)
    near_fin_row = spread(near_fin)

    def respond(slot, d):
        rows = rows_in(slot)
        return orb[at(d), rows, :] * (
            near_img_row * img[at(d), rows, :] + near_fin_row * fin[at(d), rows, :])

    def late_copy(slot):
        return pltpu.make_async_remote_copy(
            src_ref=ship_late.at[slot], dst_ref=land_late.at[slot],
            send_sem=late_s.at[slot], recv_sem=late_r.at[slot],
            device_id={"orb": quarters[slot]}, device_id_type=pl.DeviceIdType.MESH)

    for slot in range(3):
        for d in range(late):
            ship_late[slot, d] = respond(slot, d)
        tell(slot).start()
        late_copy(slot).start()

    @pl.when(has_slow)
    def _():
        slow_sent(0).wait_send()

    fast_sent(0)
    sol_src = spread(step0 + step1 * keep)
    sol_two = spread(step1 * step0)

    def solve(p, carry):
        def step(s, inner):
            rows = rows_of(s, wide)
            src[p, rows, :] = sol_src * src[p, rows, :] - sol_two * two[p, rows, :]
            return inner

        return over(step, carry)

    lax.fori_loop(0, planes, solve, 0)
    for d in range(planes):
        dens[at(d)] = respond(3, d)
    for slot in range(3):
        tell(slot).wait_recv()
    for batch, (d, count) in enumerate(batches[0]):
        for slot in range(3):
            ship_copy(0, slot, d, count, batch).wait_recv()
    for batch, (d, count) in enumerate(batches[1]):
        for slot in range(3):
            ship_copy(1, slot, d, count, batch).wait_recv()
        for e in range(d, d + count):
            total = dens[at(e)]
            for slot in range(3):
                for field in range(2):
                    total = total + mix[slot, field, 0:1, :] * land[field, slot, e - late]
            dens[at(e)] = total
    for slot in range(3):
        late_copy(slot).wait_recv()
    for d in range(late):
        dens[at(d)] = dens[at(d)] + (land_late[0, d] + land_late[1, d] + land_late[2, d])

    @pl.when(has_slow)
    def _():
        slow_sent(1).wait_send()
        slow_sent(2).wait_send()

    fast_sent(1)
    fast_sent(2)
    for r in range(3):
        exchanged(r).wait_send()
    pltpu.make_async_remote_copy(
        src_ref=ship, dst_ref=land, send_sem=ship_s, recv_sem=ship_r.at[0, 0, 0],
        device_id={"orb": both}, device_id_type=pl.DeviceIdType.MESH).wait_send()
    for slot in range(3):
        tell(slot).wait_send()
        late_copy(slot).wait_send()


def write_out(sol, den, sol_hbm, den_hbm, sem):
    planes = sol.shape[0]
    cuts = [planes * i // 4 for i in range(5)]
    copies = [
        pltpu.make_async_copy(sol.at[pl.ds(a, b - a)], sol_hbm.at[pl.ds(a, b - a)], sem.at[i])
        for i, (a, b) in enumerate(zip(cuts, cuts[1:]))
    ]
    copies.append(pltpu.make_async_copy(den, den_hbm, sem.at[4]))
    for copy in copies:
        copy.start()
    for copy in copies:
        copy.wait()


def body(n, groups, orbitals, potential, trial_potential, eigenvalues, frequency):
    count, planes, ny, nz = orbitals.shape
    assert count == 1 and groups == 4 and n % 2 == 0
    assert planes >= 2 * REACH
    assert ny % 32 == 0 and nz % 128 == 0 and min(ny, nz) > 2 * REACH
    quarter = ny // groups
    late = REACH // 3
    early = planes - late
    f32 = jnp.float32
    field = pltpu.VMEM((planes, ny, nz), f32)
    dma = pltpu.SemaphoreType.DMA
    anywhere = pl.BlockSpec(memory_space=pl.ANY)
    hbm = pl.BlockSpec(memory_space=pltpu.HBM)
    vmem = pl.BlockSpec(memory_space=pltpu.VMEM)
    sol, den = pl.pallas_call(
        functools.partial(kernel, n),
        out_shape=(
            pltpu.VMEM((planes, ny, nz), f32),
            pltpu.VMEM((planes, quarter, nz), f32),
        ),
        in_specs=[hbm] * 5,
        out_specs=(vmem, vmem),
        scratch_shapes=[field] * 6 + [
            pltpu.VMEM((2, nz, nz), jnp.bfloat16),
            pltpu.VMEM((2, ny, ny), jnp.bfloat16),
            pltpu.VMEM((3, REACH, ny, nz), f32),
            pltpu.VMEM((3, REACH, ny, nz), f32),
            pltpu.VMEM((3, n, 2, 128), f32),
            pltpu.VMEM((2, 3, early, quarter, nz), f32),
            pltpu.VMEM((2, 3, early, quarter, nz), f32),
            pltpu.VMEM((3, late, quarter, nz), f32),
            pltpu.VMEM((3, late, quarter, nz), f32),
            pltpu.VMEM((4, 2, 8, nz), f32),
            pltpu.SMEM((1,), f32), pltpu.SMEM((1,), f32),
            pltpu.SemaphoreType.REGULAR(((n - 1).bit_length(),)),
            dma((2, planes)), dma((3,)),
            dma((3,)), dma((3, REACH)), dma((3,)), dma((3, 2)), dma((3,)), dma((3,)),
            dma(()), dma((2, 3, 2 + REACH)), dma((3,)), dma((3,)), dma((3,)), dma((3,)),
        ],
        compiler_params=pltpu.CompilerParams(
            collective_id=0, has_side_effects=True, vmem_limit_bytes=50 * 2**20),
        name="sternheimer",
    )(
        orbitals.reshape(planes, ny, nz), potential, trial_potential,
        eigenvalues, frequency,
    )
    sol, den = pl.pallas_call(
        write_out,
        out_shape=(jax.ShapeDtypeStruct(sol.shape, f32), jax.ShapeDtypeStruct(den.shape, f32)),
        in_specs=[vmem] * 2,
        out_specs=(anywhere, anywhere),
        scratch_shapes=[dma((5,))],
        compiler_params=pltpu.CompilerParams(vmem_limit_bytes=2**20),
        name="write_out",
    )(sol, den)
    return sol.reshape(orbitals.shape), den


def solution(mesh):
    in_specs = (
        P("orb", "grid", None, None),
        P("grid", None, None),
        P("grid", None, None),
        P("orb"),
        P(),
    )
    out_specs = (P("orb", "grid", None, None), P("grid", "orb", None))
    call = functools.partial(body, mesh.shape["grid"], mesh.shape["orb"])
    return jax.shard_map(call, mesh=mesh, in_specs=in_specs, out_specs=out_specs, check_vma=False)
```

```python
import functools

import jax
import jax.numpy as jnp
from jax import lax
from jax.experimental import pallas as pl
from jax.experimental.pallas import tpu as pltpu
from jax.sharding import PartitionSpec as P

STENCIL = (
    -5369.0 / 1800.0,
    12.0 / 7.0,
    -15.0 / 56.0,
    10.0 / 189.0,
    -1.0 / 112.0,
    2.0 / 1925.0,
    -1.0 / 16632.0,
)
SPACING = 0.75
REACH = len(STENCIL) - 1
COEFS = tuple(-0.5 / (SPACING * SPACING) * c for c in STENCIL)
STRIP = 8


def circulant(ref, count):
    size = ref.shape[1]

    def step(s, carry):
        rows = pl.ds(pl.multiple_of(s * count, count), count)
        row = s * count + lax.broadcasted_iota(jnp.int32, (count, size), 0)
        apart = jnp.abs(row - lax.broadcasted_iota(jnp.int32, (count, size), 1))
        apart = jnp.minimum(apart, size - apart)
        full = jnp.zeros((count, size), jnp.float32)
        for k in range(1, REACH + 1):
            full = jnp.where(apart == k, COEFS[k], full)
        high = full.astype(jnp.bfloat16)
        ref[0, rows, :] = high
        ref[1, rows, :] = (full - high.astype(jnp.float32)).astype(jnp.bfloat16)
        return carry

    lax.fori_loop(0, size // count, step, 0)


def kernel(
    n,
    orb_hbm, pot_hbm, tri_hbm, eig_hbm, freq_hbm,
    src, dens,
    orb, pot, tri, img, two, fin, cz, cy,
    hslow, hfast, sums, ship, land, ship_late, land_late, mix,
    eig, freq, met, ld_sem, mat_sem,
    slow_s, slow_r, fast_s, fast_r, sum_s, sum_r,
    ship_s, ship_r, late_s, late_r, mix_s, mix_r,
):
    planes, ny, nz = src.shape
    wide = 32
    late = ship_late.shape[1]
    quarter = ship.shape[3]
    g = lax.axis_index("grid")
    o = lax.axis_index("orb")
    odd = lax.rem(g, 2)
    slow_id = lax.rem(g + n - 1 + 2 * odd, n)
    fast_id = g + 1 - 2 * odd
    has_slow = jnp.logical_and(g + odd > 0, g + odd < n)
    flip1 = o + 1 - 2 * lax.rem(o, 2)
    flip2 = lax.rem(o + 2, 4)
    first = (1 - odd) * flip1 + odd * flip2
    second = odd * flip1 + (1 - odd) * flip2
    both = 3 - o
    quarters = (both, first, second, o)

    barrier = pltpu.get_barrier_semaphore()
    @pl.when(has_slow)
    def _():
        pl.semaphore_signal(barrier, inc=1, device_id={"grid": slow_id})

    pl.semaphore_signal(barrier, inc=1, device_id={"grid": fast_id})
    for slot in range(3):
        pl.semaphore_signal(barrier, inc=1, device_id={"orb": quarters[slot]})

    half = REACH // 2
    lead = [REACH - 1, REACH - 2]
    rest = list(range(REACH - 2))
    first_group = list(range(REACH - late))
    arrivals = (
        [first_group] + [[k] for k in range(REACH - late, REACH)],
        [[*lead, 0]] + [[k] for k in rest[1:]],
        [[*lead, 0]] + [[k] for k in rest[1:]],
    )

    def at(d):
        return d + odd * (planes - 1 - 2 * d)

    def span(d, count):
        return pl.ds(d + odd * (planes - count - 2 * d), count)

    def meet(i):
        reach = 2 ** i
        for peer in (g - reach, g + reach):
            @pl.when(jnp.logical_and(peer >= 0, peer < n))
            def _():
                pl.semaphore_signal(met.at[i], inc=1, device_id={"grid": peer})

    def met_by(i):
        reach = 2 ** i
        pl.semaphore_wait(
            met.at[i], jnp.where(g >= reach, 1, 0) + jnp.where(g + reach < n, 1, 0))

    rounds = met.shape[0]

    order = list(range(REACH)) + list(range(planes - 1, REACH - 1, -1))
    groups = [(d, 2) for d in range(0, REACH, 2)]
    groups += [(planes - half, half), (REACH, planes - REACH - half)]

    def load(i):
        piece = span(*groups[i])
        return [
            pltpu.make_async_copy(hbm.at[piece], ref.at[piece], ld_sem.at[i])
            for hbm, ref in ((orb_hbm, orb), (tri_hbm, tri))
        ]

    def loaded(d):
        for i, (low, count) in enumerate(groups):
            if d == (low if low < REACH else low + count - 1):
                piece = pl.ds(0, 2 * count)
                pltpu.make_async_copy(orb_hbm.at[piece], orb.at[piece], ld_sem.at[i]).wait()

    for i in range(len(groups)):
        for copy in load(i):
            copy.start()
    mats = [
        pltpu.make_async_copy(pot_hbm, pot, mat_sem.at[0]),
        pltpu.make_async_copy(eig_hbm, eig, mat_sem.at[1]),
        pltpu.make_async_copy(freq_hbm, freq, mat_sem.at[2]),
    ]
    for copy in mats:
        copy.start()

    fields = (src, img, two)

    def slow(r, k):
        group = [i for i, ks in enumerate(arrivals[r]) if k in ks][0]
        return pltpu.make_async_remote_copy(
            src_ref=fields[r].at[at(k)], dst_ref=hslow.at[r, k],
            send_sem=slow_s.at[min(r, 1)], recv_sem=slow_r.at[r, group],
            device_id={"grid": slow_id}, device_id_type=pl.DeviceIdType.MESH)

    def slow_wait(r, ks):
        group = arrivals[r].index(ks)
        piece = hslow.at[r, pl.ds(0, len(ks))]
        pltpu.make_async_remote_copy(
            src_ref=piece, dst_ref=piece,
            send_sem=slow_s.at[min(r, 1)], recv_sem=slow_r.at[r, group],
            device_id={"grid": slow_id}, device_id_type=pl.DeviceIdType.MESH).wait_recv()

    def sent(low, count, buffer, sem):
        piece = buffer.at[pl.ds(low, count)]
        pltpu.make_async_remote_copy(
            src_ref=piece, dst_ref=piece, send_sem=sem, recv_sem=slow_r.at[0, 0],
            device_id={"grid": fast_id}, device_id_type=pl.DeviceIdType.MESH).wait_send()

    def fast(r, i):
        return pltpu.make_async_remote_copy(
            src_ref=fields[r].at[span(planes - half * (i + 1), half)],
            dst_ref=hfast.at[r, pl.ds(half * (1 - i) + odd * half * (2 * i - 1), half)],
            send_sem=fast_s.at[min(r, 1)], recv_sem=fast_r.at[i],
            device_id={"grid": fast_id}, device_id_type=pl.DeviceIdType.MESH)

    def fast_both(r):
        return pltpu.make_async_remote_copy(
            src_ref=fields[r].at[span(planes - REACH, REACH)], dst_ref=hfast.at[r],
            send_sem=fast_s.at[1], recv_sem=fast_r.at[1 + r],
            device_id={"grid": fast_id}, device_id_type=pl.DeviceIdType.MESH)

    def send(r, *ks):
        @pl.when(has_slow)
        def _():
            for k in ks:
                slow(r, k).start()

    def rows_in(slot):
        return pl.ds(pl.multiple_of(quarters[slot] * quarter, 8), quarter)

    def rows_of(s, count):
        return pl.ds(pl.multiple_of(s * count, count), count)

    def over(step, init, count=wide):
        return lax.fori_loop(0, ny // count, step, init)

    def ship_copy(field, slot, d, count, sem):
        piece = pl.ds(d - late, count)
        return pltpu.make_async_remote_copy(
            src_ref=ship.at[field, slot, piece], dst_ref=land.at[field, slot, piece],
            send_sem=ship_s, recv_sem=ship_r.at[field, sem],
            device_id={"orb": quarters[slot]}, device_id_type=pl.DeviceIdType.MESH)

    def ship_wait(field, d, count, sem):
        piece = pl.ds(d - late, count)
        pltpu.make_async_remote_copy(
            src_ref=ship.at[field, pl.ds(0, 3), piece], dst_ref=land.at[field, pl.ds(0, 3), piece],
            send_sem=ship_s, recv_sem=ship_r.at[field, sem],
            device_id={"orb": both}, device_id_type=pl.DeviceIdType.MESH).wait_recv()

    cut = 2 * REACH - half
    batches = (
        ((REACH, half), (REACH + half, planes - REACH - half), (late, REACH - late)),
        ((2 * REACH - 1, planes - 2 * REACH + 1),)
        + tuple((d, 1) for d in range(2 * REACH - 2, cut - 1, -1))
        + ((REACH, cut - REACH),)
        + tuple((d, 1) for d in range(REACH - 1, late - 1, -1)),
    )

    def share(field, value, batch):
        d, count = batches[field][batch]
        for slot in range(3):
            rows = rows_in(slot)
            for e in range(d, d + count):
                ship[field, slot, e - late] = orb[at(e), rows, :] * value[at(e), rows, :]
            ship_copy(field, slot, d, count, batch).start()

    zero = jnp.zeros((wide, nz), jnp.float32)

    def arrive(r, ks, acc):
        @pl.when(has_slow)
        def _():
            slow_wait(r, ks)

            def step(s, carry):
                rows = rows_of(s, wide)
                values = [hslow[r, k, rows, :] for k in ks]
                for d in range(REACH):
                    terms = [COEFS[d + 1 + k] * v for k, v in zip(ks, values) if d + k < REACH]
                    if terms:
                        acc[at(d), rows, :] = acc[at(d), rows, :] + functools.reduce(jnp.add, terms)
                return carry

            over(step, 0)

    def square_of(ref, d, total):
        def step(s, carry):
            value = ref[at(d), rows_of(s, wide), :]
            return carry + value * value

        return over(step, total)

    def across(value, out, low, high):
        def plane(d):
            p = at(d)
            whole = value[p]
            high_part = whole.astype(jnp.bfloat16)
            low_part = (whole - high_part.astype(jnp.float32)).astype(jnp.bfloat16)
            product = functools.partial(jnp.dot, preferred_element_type=jnp.float32)
            along_z = product(high_part, cz[0]) + product(low_part, cz[0]) + product(high_part, cz[1])
            along_y = product(cy[0], high_part) + product(cy[0], low_part) + product(cy[1], high_part)
            out[p] = along_z + along_y

        count = high - low
        size = max(k for k in range(1, REACH + 1) if count % k == 0)

        def group(i, carry):
            for j in range(size):
                plane(low + i * size + j)
            return carry

        lax.fori_loop(0, count // size, group, 0)

    def along(r, value, out, low, high):
        for side in (0, 1):
            @pl.when(odd == side)
            def _(side=side):
                def place(d):
                    return planes - 1 - d if side else d

                def part(d, rows):
                    if d < planes:
                        return value[place(d), rows, :]
                    k = d - planes
                    return hfast[r, REACH - 1 - k if side else k, rows, :]

                def strip(s, carry):
                    rows = rows_of(s, STRIP)
                    parts = {
                        d: part(d, rows)
                        for d in range(max(0, low - REACH), min(planes, high) + REACH)
                        if d < high + REACH
                    }
                    for d in range(low, high):
                        here = out.at[place(d), rows, :]
                        total = here[...] + (pot[place(d), rows, :] + (3.0 * COEFS[0] - energy)) * parts[d]
                        for k in range(1, REACH + 1):
                            near = [parts[e] for e in (d - k, d + k) if e in parts]
                            total = total + COEFS[k] * (near[0] + near[1] if len(near) == 2 else near[0])
                        here[...] = total
                    return carry

                over(strip, 0, STRIP)

    def fold(total):
        total = functools.reduce(
            lambda a, b: a + b, [total[i:i + 8] for i in range(0, wide, 8)])
        total = functools.reduce(
            lambda a, b: a + b, [total[:, i:i + 128] for i in range(0, nz, 128)])
        return jnp.sum(total, axis=0, keepdims=True)

    def exchange(r, j, slot):
        return pltpu.make_async_remote_copy(
            src_ref=sums.at[r, slot], dst_ref=sums.at[r, slot],
            send_sem=sum_s, recv_sem=sum_r.at[r],
            device_id={"grid": lax.rem(g + j, n)}, device_id_type=pl.DeviceIdType.MESH)

    def exchanged(r):
        return pltpu.make_async_remote_copy(
            src_ref=sums.at[r, pl.ds(0, n - 1)], dst_ref=sums.at[r, pl.ds(0, n - 1)],
            send_sem=sum_s, recv_sem=sum_r.at[r],
            device_id={"grid": fast_id}, device_id_type=pl.DeviceIdType.MESH)

    def post(r, *totals):
        for i in range(2):
            row = fold(totals[i]) if i < len(totals) else jnp.zeros((1, 128), jnp.float32)
            sums[r, g, i:i + 1, :] = row
        for j in range(1, n):
            exchange(r, j, g).start()

    def collect(r):
        exchanged(r).wait_recv()
        total = sums[r, 0]
        for m in range(1, n):
            total = total + sums[r, m]
        return tuple(jnp.sum(total[i:i + 1], keepdims=True) for i in range(2))

    def spread(value):
        return jnp.broadcast_to(value, (1, nz))

    circulant(cz, 32)
    circulant(cy, 32)

    total_src = zero
    for d in order:
        loaded(d)

        def step(s, carry, d=d):
            rows = rows_of(s, wide)
            value = orb[at(d), rows, :] * tri[at(d), rows, :]
            src[at(d), rows, :] = value
            return carry + value * value

        total_src = over(step, total_src)
        if d == order[0]:
            pl.semaphore_wait(barrier, 4 + has_slow.astype(jnp.int32))
            meet(0)
        if d < REACH:
            send(0, d)
        if d == planes - half:
            fast(0, 0).start()
        if d == planes - REACH:
            fast(0, 1).start()
    for copy in mats:
        copy.wait()
    energy = eig[0]
    squared = freq[0] * freq[0]

    across(src, img, REACH, REACH + half)
    fast(0, 0).wait_recv()
    along(0, src, img, REACH, REACH + half)
    share(0, img, 0)
    across(src, img, REACH + half, planes)
    if rounds > 1:
        met_by(0)
        meet(1)
    fast(0, 1).wait_recv()
    along(0, src, img, REACH + half, planes)
    fast_both(1).start()
    share(0, img, 1)
    across(src, img, 0, REACH)
    along(0, src, img, 0, REACH)
    for i in range(1, rounds - 1):
        met_by(i)
        meet(i + 1)
    total_img = zero
    for d in range(REACH, planes):
        total_img = square_of(img, d, total_img)
    early = list(range(REACH - late))
    arrive(0, early, img)
    send(1, *lead)
    share(0, img, 2)
    for k in early:
        total_img = square_of(img, REACH - 1 - k, total_img)
    across(img, two, late, planes)
    for k in range(REACH - late, REACH):
        arrive(0, [k], img)
        total_img = square_of(img, REACH - 1 - k, total_img)
        if k < REACH - 1:
            across(img, two, REACH - 1 - k, REACH - k)
    met_by(rounds - 1)
    post(0, total_src, total_img)
    send(1, *rest)
    across(img, two, 0, 1)
    fast_both(1).wait_recv()
    along(1, img, two, 0, planes)
    fast_both(2).start()

    across(two, fin, REACH, planes)
    fast_both(2).wait_recv()
    arrive(1, [*lead, 0], two)
    send(2, REACH - 1)
    across(two, fin, REACH - 1, REACH)
    along(2, two, fin, 2 * REACH - 1, planes)
    share(1, fin, 0)
    norm0, form0 = collect(0)
    step0 = norm0 / (form0 + squared * norm0)
    back = spread(1.0 - step0 * squared)
    step0_row = spread(step0)

    def square_res(d, total):
        def step(s, carry):
            rows = rows_of(s, wide)
            value = back * src[at(d), rows, :] - step0_row * two[at(d), rows, :]
            return carry + value * value

        return over(step, total)

    total_res = zero
    for d in range(REACH - 1, planes):
        total_res = square_res(d, total_res)
    for k in range(1, half):
        arrive(1, [k], two)
        d = REACH - 1 - k
        if d in lead:
            send(2, d)
        across(two, fin, d, d + 1)
        along(2, two, fin, REACH + d, REACH + d + 1)
        share(1, fin, k)
        total_res = square_res(d, total_res)
    for k in range(half, rest[-1] + 1):
        arrive(1, [k], two)
    for d in range(half):
        total_res = square_res(d, total_res)
    post(1, total_res)
    send(2, *rest)
    across(two, fin, 0, half)
    along(2, two, fin, 0, cut)
    share(1, fin, half)
    arrive(2, [*lead, 0], fin)
    share(1, fin, half + 1)

    norm1, _ = collect(1)
    ratio = norm1 / norm0
    keep = 1.0 - step0 * squared + ratio
    keep_row = spread(keep)

    def square_dir(d, total):
        def step(s, carry):
            rows = rows_of(s, wide)
            value = keep_row * src[at(d), rows, :] - step0_row * two[at(d), rows, :]
            return carry + value * value

        return over(step, total)

    def square_fin(d, total):
        def step(s, carry):
            rows = rows_of(s, wide)
            value = keep_row * img[at(d), rows, :] - step0_row * fin[at(d), rows, :]
            return carry + value * value

        return over(step, total)

    def loop_over(low, high, body, total):
        return lax.fori_loop(low, high, body, total)

    total_dir = loop_over(0, planes, square_dir, zero)
    total_fin = loop_over(REACH - 1, planes, square_fin, zero)
    for k in rest[1:]:
        arrive(2, [k], fin)
        d = REACH - 1 - k
        if k < rest[-1]:
            share(1, fin, half + 1 + k)
            total_fin = square_fin(d, total_fin)
    for d in range(REACH - rest[-1]):
        total_fin = square_fin(d, total_fin)
    post(2, total_dir, total_fin)
    for k in range(rest[-1], REACH - late):
        share(1, fin, half + 1 + k)
    form_dir, form_fin = collect(2)
    step1 = norm1 / (form_fin + squared * form_dir)

    near_img = -4.0 * (step0 + step1 * keep)
    near_fin = 4.0 * (step1 * step0)
    mix[3, 0] = jnp.broadcast_to(near_img, mix.shape[2:])
    mix[3, 1] = jnp.broadcast_to(near_fin, mix.shape[2:])

    def tell(slot):
        return pltpu.make_async_remote_copy(
            src_ref=mix.at[3], dst_ref=mix.at[slot],
            send_sem=mix_s, recv_sem=mix_r,
            device_id={"orb": quarters[slot]}, device_id_type=pl.DeviceIdType.MESH)

    near_img_row = spread(near_img)
    near_fin_row = spread(near_fin)

    def respond(slot, d):
        rows = rows_in(slot)
        return orb[at(d), rows, :] * (
            near_img_row * img[at(d), rows, :] + near_fin_row * fin[at(d), rows, :])

    def all_of(source, target, send, recv):
        return pltpu.make_async_remote_copy(
            src_ref=source, dst_ref=target, send_sem=send, recv_sem=recv,
            device_id={"orb": both}, device_id_type=pl.DeviceIdType.MESH)

    told = all_of(mix.at[pl.ds(0, 3)], mix.at[pl.ds(0, 3)], mix_s, mix_r)
    late_all = all_of(ship_late, land_late, late_s, late_r)

    def late_copy(slot):
        return pltpu.make_async_remote_copy(
            src_ref=ship_late.at[slot], dst_ref=land_late.at[slot],
            send_sem=late_s, recv_sem=late_r,
            device_id={"orb": quarters[slot]}, device_id_type=pl.DeviceIdType.MESH)

    for slot in range(3):
        for d in range(late):
            ship_late[slot, d] = respond(slot, d)
        tell(slot).start()
        late_copy(slot).start()

    @pl.when(has_slow)
    def _():
        sent(0, 1, hslow, slow_s.at[0])

    sent(0, 1, hfast, fast_s.at[0])
    sol_src = spread(step0 + step1 * keep)
    sol_two = spread(step1 * step0)

    def solve(p, carry):
        def step(s, inner):
            rows = rows_of(s, wide)
            src[p, rows, :] = sol_src * src[p, rows, :] - sol_two * two[p, rows, :]
            return inner

        return over(step, carry)

    lax.fori_loop(0, planes, solve, 0)
    for d in range(planes):
        dens[at(d)] = respond(3, d)
    told.wait_recv()
    for batch, (d, count) in enumerate(batches[0]):
        ship_wait(0, d, count, batch)
    for batch, (d, count) in enumerate(batches[1]):
        ship_wait(1, d, count, batch)
        for e in range(d, d + count):
            total = dens[at(e)]
            for slot in range(3):
                for field in range(2):
                    total = total + mix[slot, field, 0:1, :] * land[field, slot, e - late]
            dens[at(e)] = total
    late_all.wait_recv()
    for d in range(late):
        dens[at(d)] = dens[at(d)] + (land_late[0, d] + land_late[1, d] + land_late[2, d])

    @pl.when(has_slow)
    def _():
        sent(1, 2, hslow, slow_s.at[1])

    sent(1, 2, hfast, fast_s.at[1])
    all_of(
        sums.at[pl.ds(0, 3), pl.ds(0, n - 1)], sums.at[pl.ds(0, 3), pl.ds(0, n - 1)],
        sum_s, sum_r.at[0]).wait_send()
    all_of(ship, land, ship_s, ship_r.at[0, 0]).wait_send()
    told.wait_send()
    late_all.wait_send()


def write_out(sol, den, sol_hbm, den_hbm, sem):
    planes = sol.shape[0]
    cuts = [planes * i // 4 for i in range(5)]
    copies = [
        pltpu.make_async_copy(sol.at[pl.ds(a, b - a)], sol_hbm.at[pl.ds(a, b - a)], sem.at[i])
        for i, (a, b) in enumerate(zip(cuts, cuts[1:]))
    ]
    copies.append(pltpu.make_async_copy(den, den_hbm, sem.at[4]))
    for copy in copies:
        copy.start()
    for copy in copies:
        copy.wait()


def body(n, groups, orbitals, potential, trial_potential, eigenvalues, frequency):
    count, planes, ny, nz = orbitals.shape
    assert count == 1 and groups == 4 and n % 2 == 0
    assert planes >= 2 * REACH
    assert ny % 32 == 0 and nz % 128 == 0 and min(ny, nz) > 2 * REACH
    quarter = ny // groups
    late = REACH // 3
    early = planes - late
    f32 = jnp.float32
    field = pltpu.VMEM((planes, ny, nz), f32)
    dma = pltpu.SemaphoreType.DMA
    anywhere = pl.BlockSpec(memory_space=pl.ANY)
    hbm = pl.BlockSpec(memory_space=pltpu.HBM)
    vmem = pl.BlockSpec(memory_space=pltpu.VMEM)
    sol, den = pl.pallas_call(
        functools.partial(kernel, n),
        out_shape=(
            pltpu.VMEM((planes, ny, nz), f32),
            pltpu.VMEM((planes, quarter, nz), f32),
        ),
        in_specs=[hbm] * 5,
        out_specs=(vmem, vmem),
        scratch_shapes=[field] * 6 + [
            pltpu.VMEM((2, nz, nz), jnp.bfloat16),
            pltpu.VMEM((2, ny, ny), jnp.bfloat16),
            pltpu.VMEM((3, REACH, ny, nz), f32),
            pltpu.VMEM((3, REACH, ny, nz), f32),
            pltpu.VMEM((3, n, 2, 128), f32),
            pltpu.VMEM((2, 3, early, quarter, nz), f32),
            pltpu.VMEM((2, 3, early, quarter, nz), f32),
            pltpu.VMEM((3, late, quarter, nz), f32),
            pltpu.VMEM((3, late, quarter, nz), f32),
            pltpu.VMEM((4, 2, 8, nz), f32),
            pltpu.SMEM((1,), f32), pltpu.SMEM((1,), f32),
            pltpu.SemaphoreType.REGULAR(((n - 1).bit_length(),)),
            dma((2 + REACH // 2,)), dma((3,)),
            dma((2,)), dma((3, max(1 + late, REACH - 2))), dma((2,)), dma((4,)), dma(()), dma((3,)),
            dma(()), dma((2, 2 + REACH)), dma(()), dma(()), dma(()), dma(()),
        ],
        compiler_params=pltpu.CompilerParams(
            collective_id=0, has_side_effects=True, vmem_limit_bytes=50 * 2**20),
        name="sternheimer",
    )(
        orbitals.reshape(planes, ny, nz), potential, trial_potential,
        eigenvalues, frequency,
    )
    sol, den = pl.pallas_call(
        write_out,
        out_shape=(jax.ShapeDtypeStruct(sol.shape, f32), jax.ShapeDtypeStruct(den.shape, f32)),
        in_specs=[vmem] * 2,
        out_specs=(anywhere, anywhere),
        scratch_shapes=[dma((5,))],
        compiler_params=pltpu.CompilerParams(vmem_limit_bytes=2**20),
        name="write_out",
    )(sol, den)
    return sol.reshape(orbitals.shape), den


def solution(mesh):
    in_specs = (
        P("orb", "grid", None, None),
        P("grid", None, None),
        P("grid", None, None),
        P("orb"),
        P(),
    )
    out_specs = (P("orb", "grid", None, None), P("grid", "orb", None))
    call = functools.partial(body, mesh.shape["grid"], mesh.shape["orb"])
    return jax.shard_map(call, mesh=mesh, in_specs=in_specs, out_specs=out_specs, check_vma=False)
```

```python
import functools

import jax
import jax.numpy as jnp
from jax import lax
from jax.experimental import pallas as pl
from jax.experimental.pallas import tpu as pltpu
from jax.sharding import PartitionSpec as P

STENCIL = (
    -5369.0 / 1800.0,
    12.0 / 7.0,
    -15.0 / 56.0,
    10.0 / 189.0,
    -1.0 / 112.0,
    2.0 / 1925.0,
    -1.0 / 16632.0,
)
SPACING = 0.75
REACH = len(STENCIL) - 1
COEFS = tuple(-0.5 / (SPACING * SPACING) * c for c in STENCIL)
STRIP = 8


def circulant(ref, count):
    size = ref.shape[1]

    def step(s, carry):
        rows = pl.ds(pl.multiple_of(s * count, count), count)
        row = s * count + lax.broadcasted_iota(jnp.int32, (count, size), 0)
        apart = jnp.abs(row - lax.broadcasted_iota(jnp.int32, (count, size), 1))
        apart = jnp.minimum(apart, size - apart)
        full = jnp.zeros((count, size), jnp.float32)
        for k in range(1, REACH + 1):
            full = jnp.where(apart == k, COEFS[k], full)
        high = full.astype(jnp.bfloat16)
        ref[0, rows, :] = high
        ref[1, rows, :] = (full - high.astype(jnp.float32)).astype(jnp.bfloat16)
        return carry

    lax.fori_loop(0, size // count, step, 0)


def kernel(
    n,
    orb_hbm, pot_hbm, tri_hbm, eig_hbm, freq_hbm,
    src, dens,
    orb, pot, tri, img, two, fin, cz, cy,
    hslow, hfast, sums, ship, land, ship_late, land_late, mix,
    eig, freq, met, ld_sem, mat_sem,
    slow_s, slow_r, fast_s, fast_r, sum_s, sum_r,
    ship_s, ship_r, late_s, late_r, mix_s, mix_r,
):
    planes, ny, nz = src.shape
    wide = 32
    late = ship_late.shape[1]
    quarter = ship.shape[3]
    g = lax.axis_index("grid")
    o = lax.axis_index("orb")
    odd = lax.rem(g, 2)
    slow_id = lax.rem(g + n - 1 + 2 * odd, n)
    fast_id = g + 1 - 2 * odd
    has_slow = jnp.logical_and(g + odd > 0, g + odd < n)
    flip1 = o + 1 - 2 * lax.rem(o, 2)
    flip2 = lax.rem(o + 2, 4)
    first = (1 - odd) * flip1 + odd * flip2
    second = odd * flip1 + (1 - odd) * flip2
    both = 3 - o
    quarters = (both, first, second, o)

    barrier = pltpu.get_barrier_semaphore()
    @pl.when(has_slow)
    def _():
        pl.semaphore_signal(barrier, inc=1, device_id={"grid": slow_id})

    pl.semaphore_signal(barrier, inc=1, device_id={"grid": fast_id})
    for slot in (1, 2):
        pl.semaphore_signal(barrier, inc=1, device_id={"orb": quarters[slot]})

    half = REACH // 2
    lead = [REACH - 1, REACH - 2]
    rest = list(range(REACH - 2))
    first_group = list(range(REACH - late))
    arrivals = (
        [first_group] + [[k] for k in range(REACH - late, REACH)],
        [[*lead, 0]] + [[k] for k in rest[1:]],
        [[*lead, 0]] + [[k] for k in rest[1:]],
    )

    before = [sum(len(group) for group in arrivals[:r]) for r in range(3)]

    def at(d):
        return d + odd * (planes - 1 - 2 * d)

    def span(d, count):
        return pl.ds(d + odd * (planes - count - 2 * d), count)

    def meet(i):
        reach = 2 ** i
        for peer in (g - reach, g + reach):
            @pl.when(jnp.logical_and(peer >= 0, peer < n))
            def _():
                pl.semaphore_signal(met.at[i], inc=1, device_id={"grid": peer})

    def met_by(i):
        reach = 2 ** i
        pl.semaphore_wait(
            met.at[i], jnp.where(g >= reach, 1, 0) + jnp.where(g + reach < n, 1, 0))

    rounds = met.shape[0] - 1

    order = list(range(REACH)) + list(range(planes - 1, REACH - 1, -1))
    groups = [(d, 2) for d in range(0, REACH, 2)]
    groups += [(planes - half, half), (REACH, planes - REACH - half)]

    def load(i):
        piece = span(*groups[i])
        return [
            pltpu.make_async_copy(hbm.at[piece], ref.at[piece], ld_sem.at[i])
            for hbm, ref in ((orb_hbm, orb), (tri_hbm, tri))
        ]

    def loaded(d):
        for i, (low, count) in enumerate(groups):
            if d == (low if low < REACH else low + count - 1):
                piece = pl.ds(0, 2 * count)
                pltpu.make_async_copy(orb_hbm.at[piece], orb.at[piece], ld_sem.at[i]).wait()

    for i in range(len(groups)):
        for copy in load(i):
            copy.start()
    mats = [
        pltpu.make_async_copy(pot_hbm, pot, mat_sem.at[0]),
        pltpu.make_async_copy(eig_hbm, eig, mat_sem.at[1]),
        pltpu.make_async_copy(freq_hbm, freq, mat_sem.at[2]),
    ]
    for copy in mats:
        copy.start()

    fields = (src, img, two)

    def slow(r, k):
        group = [i for i, ks in enumerate(arrivals[r]) if k in ks][0]
        return pltpu.make_async_remote_copy(
            src_ref=fields[r].at[at(k)], dst_ref=hslow.at[r, k],
            send_sem=slow_s.at[min(r, 1)], recv_sem=slow_r.at[before[r] + group],
            device_id={"grid": slow_id}, device_id_type=pl.DeviceIdType.MESH)

    def slow_wait(r, ks):
        group = arrivals[r].index(ks)
        piece = hslow.at[r, pl.ds(0, len(ks))]
        pltpu.make_async_remote_copy(
            src_ref=piece, dst_ref=piece,
            send_sem=slow_s.at[min(r, 1)], recv_sem=slow_r.at[before[r] + group],
            device_id={"grid": slow_id}, device_id_type=pl.DeviceIdType.MESH).wait_recv()

    def sent(low, count, buffer, sem):
        piece = buffer.at[pl.ds(low, count)]
        pltpu.make_async_remote_copy(
            src_ref=piece, dst_ref=piece, send_sem=sem, recv_sem=slow_r.at[0],
            device_id={"grid": fast_id}, device_id_type=pl.DeviceIdType.MESH).wait_send()

    def fast(r, i):
        return pltpu.make_async_remote_copy(
            src_ref=fields[r].at[span(planes - half * (i + 1), half)],
            dst_ref=hfast.at[r, pl.ds(half * (1 - i) + odd * half * (2 * i - 1), half)],
            send_sem=fast_s.at[min(r, 1)], recv_sem=fast_r.at[i],
            device_id={"grid": fast_id}, device_id_type=pl.DeviceIdType.MESH)

    def fast_both(r):
        return pltpu.make_async_remote_copy(
            src_ref=fields[r].at[span(planes - REACH, REACH)], dst_ref=hfast.at[r],
            send_sem=fast_s.at[1], recv_sem=fast_r.at[1 + r],
            device_id={"grid": fast_id}, device_id_type=pl.DeviceIdType.MESH)

    def send(r, *ks):
        @pl.when(has_slow)
        def _():
            for k in ks:
                slow(r, k).start()

    def rows_in(slot):
        return pl.ds(pl.multiple_of(quarters[slot] * quarter, 8), quarter)

    def rows_of(s, count):
        return pl.ds(pl.multiple_of(s * count, count), count)

    def over(step, init, count=wide):
        return lax.fori_loop(0, ny // count, step, init)

    def ship_copy(field, slot, d, count):
        piece = pl.ds(d - late, count)
        return pltpu.make_async_remote_copy(
            src_ref=ship.at[field, slot, piece], dst_ref=land.at[field, slot, piece],
            send_sem=ship_s, recv_sem=ship_r.at[field],
            device_id={"orb": quarters[slot]}, device_id_type=pl.DeviceIdType.MESH)

    def ship_wait(field):
        pltpu.make_async_remote_copy(
            src_ref=ship.at[field], dst_ref=land.at[field],
            send_sem=ship_s, recv_sem=ship_r.at[field],
            device_id={"orb": both}, device_id_type=pl.DeviceIdType.MESH).wait_recv()

    cut = 2 * REACH - half
    batches = (
        (
            (REACH, 1), (REACH + 1, half - 1), (REACH + half, planes - REACH - half),
            (late, REACH - late),
        ),
        ((2 * REACH - 1, planes - 2 * REACH + 1),)
        + tuple((d, 1) for d in range(2 * REACH - 2, cut - 1, -1))
        + ((REACH, cut - REACH),)
        + tuple((d, 1) for d in range(REACH - 1, late - 1, -1)),
    )

    def share(field, value, batch):
        d, count = batches[field][batch]
        for slot in range(3):
            rows = rows_in(slot)
            for e in range(d, d + count):
                ship[field, slot, e - late] = orb[at(e), rows, :] * value[at(e), rows, :]
            ship_copy(field, slot, d, count).start()

    zero = jnp.zeros((wide, nz), jnp.float32)

    def arrive(r, ks, acc):
        @pl.when(has_slow)
        def _():
            slow_wait(r, ks)

            def step(s, carry):
                rows = rows_of(s, wide)
                values = [hslow[r, k, rows, :] for k in ks]
                for d in range(REACH):
                    terms = [COEFS[d + 1 + k] * v for k, v in zip(ks, values) if d + k < REACH]
                    if terms:
                        acc[at(d), rows, :] = acc[at(d), rows, :] + functools.reduce(jnp.add, terms)
                return carry

            over(step, 0)

    def square_of(ref, d, total):
        def step(s, carry):
            value = ref[at(d), rows_of(s, wide), :]
            return carry + value * value

        return over(step, total)

    def across(value, out, low, high):
        def plane(d):
            p = at(d)
            whole = value[p]
            high_part = whole.astype(jnp.bfloat16)
            low_part = (whole - high_part.astype(jnp.float32)).astype(jnp.bfloat16)
            product = functools.partial(jnp.dot, preferred_element_type=jnp.float32)
            along_z = product(high_part, cz[0]) + product(low_part, cz[0]) + product(high_part, cz[1])
            along_y = product(cy[0], high_part) + product(cy[0], low_part) + product(cy[1], high_part)
            out[p] = along_z + along_y

        count = high - low
        size = max(k for k in range(1, REACH + 1) if count % k == 0)

        def group(i, carry):
            for j in range(size):
                plane(low + i * size + j)
            return carry

        lax.fori_loop(0, count // size, group, 0)

    def along(r, value, out, low, high):
        for side in (0, 1):
            @pl.when(odd == side)
            def _(side=side):
                def place(d):
                    return planes - 1 - d if side else d

                def part(d, rows):
                    if d < planes:
                        return value[place(d), rows, :]
                    k = d - planes
                    return hfast[r, REACH - 1 - k if side else k, rows, :]

                def strip(s, carry):
                    rows = rows_of(s, STRIP)
                    parts = {
                        d: part(d, rows)
                        for d in range(max(0, low - REACH), min(planes, high) + REACH)
                        if d < high + REACH
                    }
                    for d in range(low, high):
                        here = out.at[place(d), rows, :]
                        total = here[...] + (pot[place(d), rows, :] + (3.0 * COEFS[0] - energy)) * parts[d]
                        for k in range(1, REACH + 1):
                            near = [parts[e] for e in (d - k, d + k) if e in parts]
                            total = total + COEFS[k] * (near[0] + near[1] if len(near) == 2 else near[0])
                        here[...] = total
                    return carry

                over(strip, 0, STRIP)

    def fold(total):
        total = functools.reduce(
            lambda a, b: a + b, [total[i:i + 8] for i in range(0, wide, 8)])
        total = functools.reduce(
            lambda a, b: a + b, [total[:, i:i + 128] for i in range(0, nz, 128)])
        return jnp.sum(total, axis=0, keepdims=True)

    def exchange(r, j, slot):
        return pltpu.make_async_remote_copy(
            src_ref=sums.at[r, slot], dst_ref=sums.at[r, slot],
            send_sem=sum_s, recv_sem=sum_r.at[r],
            device_id={"grid": lax.rem(g + j, n)}, device_id_type=pl.DeviceIdType.MESH)

    def exchanged(r):
        return pltpu.make_async_remote_copy(
            src_ref=sums.at[r, pl.ds(0, n - 1)], dst_ref=sums.at[r, pl.ds(0, n - 1)],
            send_sem=sum_s, recv_sem=sum_r.at[r],
            device_id={"grid": fast_id}, device_id_type=pl.DeviceIdType.MESH)

    def post(r, *totals):
        for i in range(2):
            row = fold(totals[i]) if i < len(totals) else jnp.zeros((1, 128), jnp.float32)
            sums[r, g, i:i + 1, :] = row
        for j in range(1, n):
            exchange(r, j, g).start()

    def collect(r):
        exchanged(r).wait_recv()
        total = sums[r, 0]
        for m in range(1, n):
            total = total + sums[r, m]
        return tuple(jnp.sum(total[i:i + 1], keepdims=True) for i in range(2))

    def spread(value):
        return jnp.broadcast_to(value, (1, nz))

    circulant(cz, 32)
    circulant(cy, 32)

    total_src = zero
    for d in order:
        loaded(d)

        def step(s, carry, d=d):
            rows = rows_of(s, wide)
            value = orb[at(d), rows, :] * tri[at(d), rows, :]
            src[at(d), rows, :] = value
            return carry + value * value

        total_src = over(step, total_src)
        if d == order[0]:
            pl.semaphore_wait(barrier, 3 + has_slow.astype(jnp.int32))
            pl.semaphore_signal(met.at[rounds], inc=1, device_id={"orb": first})
            meet(0)
        if d < REACH:
            send(0, d)
        if d == planes - half:
            fast(0, 0).start()
        if d == planes - REACH:
            fast(0, 1).start()
    for copy in mats:
        copy.wait()
    energy = eig[0]
    squared = freq[0] * freq[0]

    across(src, img, REACH, REACH + 1)
    fast(0, 0).wait_recv()
    along(0, src, img, REACH, REACH + 1)
    pl.semaphore_wait(met.at[rounds], 1)
    share(0, img, 0)
    across(src, img, REACH + 1, REACH + half)
    along(0, src, img, REACH + 1, REACH + half)
    share(0, img, 1)
    across(src, img, REACH + half, planes)
    if rounds > 1:
        met_by(0)
        meet(1)
    fast(0, 1).wait_recv()
    along(0, src, img, REACH + half, planes)
    fast_both(1).start()
    share(0, img, 2)
    across(src, img, 0, REACH)
    along(0, src, img, 0, REACH)
    for i in range(1, rounds - 1):
        met_by(i)
        meet(i + 1)
    total_img = zero
    for d in range(REACH, planes):
        total_img = square_of(img, d, total_img)
    early = list(range(REACH - late))
    arrive(0, early, img)
    send(1, *lead)
    share(0, img, 3)
    for k in early:
        total_img = square_of(img, REACH - 1 - k, total_img)
    across(img, two, late, planes)
    for k in range(REACH - late, REACH):
        arrive(0, [k], img)
        total_img = square_of(img, REACH - 1 - k, total_img)
        if k < REACH - 1:
            across(img, two, REACH - 1 - k, REACH - k)
    met_by(rounds - 1)
    post(0, total_src, total_img)
    send(1, *rest)
    across(img, two, 0, 1)
    fast_both(1).wait_recv()
    along(1, img, two, 0, planes)
    fast_both(2).start()

    across(two, fin, REACH, planes)
    fast_both(2).wait_recv()
    arrive(1, [*lead, 0], two)
    send(2, REACH - 1)
    across(two, fin, REACH - 1, REACH)
    along(2, two, fin, 2 * REACH - 1, planes)
    share(1, fin, 0)
    norm0, form0 = collect(0)
    step0 = norm0 / (form0 + squared * norm0)
    back = spread(1.0 - step0 * squared)
    step0_row = spread(step0)

    def square_res(d, total):
        def step(s, carry):
            rows = rows_of(s, wide)
            value = back * src[at(d), rows, :] - step0_row * two[at(d), rows, :]
            return carry + value * value

        return over(step, total)

    total_res = zero
    for d in range(REACH - 1, planes):
        total_res = square_res(d, total_res)
    for k in range(1, half):
        arrive(1, [k], two)
        d = REACH - 1 - k
        if d in lead:
            send(2, d)
        across(two, fin, d, d + 1)
        along(2, two, fin, REACH + d, REACH + d + 1)
        share(1, fin, k)
        total_res = square_res(d, total_res)
    for k in range(half, rest[-1] + 1):
        arrive(1, [k], two)
    for d in range(half):
        total_res = square_res(d, total_res)
    post(1, total_res)
    send(2, *rest)
    across(two, fin, 0, half)
    along(2, two, fin, 0, cut)
    share(1, fin, half)
    arrive(2, [*lead, 0], fin)
    share(1, fin, half + 1)

    norm1, _ = collect(1)
    ratio = norm1 / norm0
    keep = 1.0 - step0 * squared + ratio
    keep_row = spread(keep)

    def square_dir(d, total):
        def step(s, carry):
            rows = rows_of(s, wide)
            value = keep_row * src[at(d), rows, :] - step0_row * two[at(d), rows, :]
            return carry + value * value

        return over(step, total)

    def square_fin(d, total):
        def step(s, carry):
            rows = rows_of(s, wide)
            value = keep_row * img[at(d), rows, :] - step0_row * fin[at(d), rows, :]
            return carry + value * value

        return over(step, total)

    def loop_over(low, high, body, total):
        return lax.fori_loop(low, high, body, total)

    total_dir = loop_over(0, planes, square_dir, zero)
    total_fin = loop_over(REACH - 1, planes, square_fin, zero)
    for k in rest[1:]:
        arrive(2, [k], fin)
        d = REACH - 1 - k
        if k < rest[-1]:
            share(1, fin, half + 1 + k)
            total_fin = square_fin(d, total_fin)
    for d in range(REACH - rest[-1]):
        total_fin = square_fin(d, total_fin)
    post(2, total_dir, total_fin)
    for k in range(rest[-1], REACH - late):
        share(1, fin, half + 1 + k)
    form_dir, form_fin = collect(2)
    step1 = norm1 / (form_fin + squared * form_dir)

    near_img = -4.0 * (step0 + step1 * keep)
    near_fin = 4.0 * (step1 * step0)
    mix[3, 0] = jnp.broadcast_to(near_img, mix.shape[2:])
    mix[3, 1] = jnp.broadcast_to(near_fin, mix.shape[2:])

    def tell(slot):
        return pltpu.make_async_remote_copy(
            src_ref=mix.at[3], dst_ref=mix.at[slot],
            send_sem=mix_s, recv_sem=mix_r,
            device_id={"orb": quarters[slot]}, device_id_type=pl.DeviceIdType.MESH)

    near_img_row = spread(near_img)
    near_fin_row = spread(near_fin)

    def respond(slot, d):
        rows = rows_in(slot)
        return orb[at(d), rows, :] * (
            near_img_row * img[at(d), rows, :] + near_fin_row * fin[at(d), rows, :])

    def all_of(source, target, send, recv):
        return pltpu.make_async_remote_copy(
            src_ref=source, dst_ref=target, send_sem=send, recv_sem=recv,
            device_id={"orb": both}, device_id_type=pl.DeviceIdType.MESH)

    told = all_of(mix.at[pl.ds(0, 3)], mix.at[pl.ds(0, 3)], mix_s, mix_r)
    late_all = all_of(ship_late, land_late, late_s, late_r)

    def late_copy(slot):
        return pltpu.make_async_remote_copy(
            src_ref=ship_late.at[slot], dst_ref=land_late.at[slot],
            send_sem=late_s, recv_sem=late_r,
            device_id={"orb": quarters[slot]}, device_id_type=pl.DeviceIdType.MESH)

    for slot in range(3):
        for d in range(late):
            ship_late[slot, d] = respond(slot, d)
        tell(slot).start()
        late_copy(slot).start()

    @pl.when(has_slow)
    def _():
        sent(0, 1, hslow, slow_s.at[0])

    sent(0, 1, hfast, fast_s.at[0])
    sol_src = spread(step0 + step1 * keep)
    sol_two = spread(step1 * step0)

    def solve(p, carry):
        def step(s, inner):
            rows = rows_of(s, wide)
            src[p, rows, :] = sol_src * src[p, rows, :] - sol_two * two[p, rows, :]
            return inner

        return over(step, carry)

    lax.fori_loop(0, planes, solve, 0)
    for d in range(planes):
        dens[at(d)] = respond(3, d)
    told.wait_recv()
    for field in range(2):
        ship_wait(field)
    for e in range(late, planes):
        total = dens[at(e)]
        for slot in range(3):
            for field in range(2):
                total = total + mix[slot, field, 0:1, :] * land[field, slot, e - late]
        dens[at(e)] = total
    late_all.wait_recv()
    for d in range(late):
        dens[at(d)] = dens[at(d)] + (land_late[0, d] + land_late[1, d] + land_late[2, d])

    @pl.when(has_slow)
    def _():
        sent(1, 2, hslow, slow_s.at[1])

    sent(1, 2, hfast, fast_s.at[1])
    all_of(
        sums.at[pl.ds(0, 3), pl.ds(0, n - 1)], sums.at[pl.ds(0, 3), pl.ds(0, n - 1)],
        sum_s, sum_r.at[0]).wait_send()
    all_of(ship, land, ship_s, ship_r.at[0]).wait_send()
    told.wait_send()
    late_all.wait_send()


def write_out(sol, den, sol_hbm, den_hbm, sem):
    planes = sol.shape[0]
    cuts = [planes * i // 4 for i in range(5)]
    copies = [
        pltpu.make_async_copy(sol.at[pl.ds(a, b - a)], sol_hbm.at[pl.ds(a, b - a)], sem.at[i])
        for i, (a, b) in enumerate(zip(cuts, cuts[1:]))
    ]
    copies.append(pltpu.make_async_copy(den, den_hbm, sem.at[4]))
    for copy in copies:
        copy.start()
    for copy in copies:
        copy.wait()


def body(n, groups, orbitals, potential, trial_potential, eigenvalues, frequency):
    count, planes, ny, nz = orbitals.shape
    assert count == 1 and groups == 4 and n % 2 == 0
    assert planes >= 2 * REACH
    assert ny % 32 == 0 and nz % 128 == 0 and min(ny, nz) > 2 * REACH
    quarter = ny // groups
    late = REACH // 3
    early = planes - late
    f32 = jnp.float32
    field = pltpu.VMEM((planes, ny, nz), f32)
    dma = pltpu.SemaphoreType.DMA
    anywhere = pl.BlockSpec(memory_space=pl.ANY)
    hbm = pl.BlockSpec(memory_space=pltpu.HBM)
    vmem = pl.BlockSpec(memory_space=pltpu.VMEM)
    sol, den = pl.pallas_call(
        functools.partial(kernel, n),
        out_shape=(
            pltpu.VMEM((planes, ny, nz), f32),
            pltpu.VMEM((planes, quarter, nz), f32),
        ),
        in_specs=[hbm] * 5,
        out_specs=(vmem, vmem),
        scratch_shapes=[field] * 6 + [
            pltpu.VMEM((2, nz, nz), jnp.bfloat16),
            pltpu.VMEM((2, ny, ny), jnp.bfloat16),
            pltpu.VMEM((3, REACH, ny, nz), f32),
            pltpu.VMEM((3, REACH, ny, nz), f32),
            pltpu.VMEM((3, n, 2, 128), f32),
            pltpu.VMEM((2, 3, early, quarter, nz), f32),
            pltpu.VMEM((2, 3, early, quarter, nz), f32),
            pltpu.VMEM((3, late, quarter, nz), f32),
            pltpu.VMEM((3, late, quarter, nz), f32),
            pltpu.VMEM((4, 2, 8, nz), f32),
            pltpu.SMEM((1,), f32), pltpu.SMEM((1,), f32),
            pltpu.SemaphoreType.REGULAR(((n - 1).bit_length() + 1,)),
            dma((2 + REACH // 2,)), dma((3,)),
            dma((2,)), dma((1 + late + 2 * (REACH - 2),)), dma((2,)), dma((4,)), dma(()), dma((3,)),
            dma(()), dma((2,)), dma(()), dma(()), dma(()), dma(()),
        ],
        compiler_params=pltpu.CompilerParams(
            collective_id=0, has_side_effects=True, vmem_limit_bytes=50 * 2**20),
        name="sternheimer",
    )(
        orbitals.reshape(planes, ny, nz), potential, trial_potential,
        eigenvalues, frequency,
    )
    sol, den = pl.pallas_call(
        write_out,
        out_shape=(jax.ShapeDtypeStruct(sol.shape, f32), jax.ShapeDtypeStruct(den.shape, f32)),
        in_specs=[vmem] * 2,
        out_specs=(anywhere, anywhere),
        scratch_shapes=[dma((5,))],
        compiler_params=pltpu.CompilerParams(vmem_limit_bytes=2**20),
        name="write_out",
    )(sol, den)
    return sol.reshape(orbitals.shape), den


def solution(mesh):
    in_specs = (
        P("orb", "grid", None, None),
        P("grid", None, None),
        P("grid", None, None),
        P("orb"),
        P(),
    )
    out_specs = (P("orb", "grid", None, None), P("grid", "orb", None))
    call = functools.partial(body, mesh.shape["grid"], mesh.shape["orb"])
    return jax.shard_map(call, mesh=mesh, in_specs=in_specs, out_specs=out_specs, check_vma=False)
```

```python
import functools

import jax
import jax.numpy as jnp
from jax import lax
from jax.experimental import pallas as pl
from jax.experimental.pallas import tpu as pltpu
from jax.sharding import PartitionSpec as P

STENCIL = (
    -5369.0 / 1800.0,
    12.0 / 7.0,
    -15.0 / 56.0,
    10.0 / 189.0,
    -1.0 / 112.0,
    2.0 / 1925.0,
    -1.0 / 16632.0,
)
SPACING = 0.75
REACH = len(STENCIL) - 1
COEFS = tuple(-0.5 / (SPACING * SPACING) * c for c in STENCIL)
STRIP = 8


def circulant(ref, count):
    size = ref.shape[1]

    def step(s, carry):
        rows = pl.ds(pl.multiple_of(s * count, count), count)
        row = s * count + lax.broadcasted_iota(jnp.int32, (count, size), 0)
        apart = jnp.abs(row - lax.broadcasted_iota(jnp.int32, (count, size), 1))
        apart = jnp.minimum(apart, size - apart)
        full = jnp.zeros((count, size), jnp.float32)
        for k in range(1, REACH + 1):
            full = jnp.where(apart == k, COEFS[k], full)
        high = full.astype(jnp.bfloat16)
        ref[0, rows, :] = high
        ref[1, rows, :] = (full - high.astype(jnp.float32)).astype(jnp.bfloat16)
        return carry

    lax.fori_loop(0, size // count, step, 0)


def kernel(
    n,
    orb_hbm, pot_hbm, tri_hbm, eig_hbm, freq_hbm,
    src, dens,
    orb, pot, tri, img, two, fin, cz, cy,
    hslow, hfast, sums, ship, land, ship_late, land_late, mix,
    eig, freq, met, ld_sem, mat_sem,
    slow_s, slow_r, fast_s, fast_r, sum_s, sum_r,
    ship_s, ship_r, late_s, late_r, mix_s, mix_r,
):
    planes, ny, nz = src.shape
    wide = 32
    late = ship_late.shape[1]
    quarter = ship.shape[3]
    g = lax.axis_index("grid")
    o = lax.axis_index("orb")
    odd = lax.rem(g, 2)
    slow_id = lax.rem(g + n - 1 + 2 * odd, n)
    fast_id = g + 1 - 2 * odd
    has_slow = jnp.logical_and(g + odd > 0, g + odd < n)
    flip1 = o + 1 - 2 * lax.rem(o, 2)
    flip2 = lax.rem(o + 2, 4)
    first = (1 - odd) * flip1 + odd * flip2
    second = odd * flip1 + (1 - odd) * flip2
    both = 3 - o
    quarters = (both, first, second, o)

    barrier = pltpu.get_barrier_semaphore()
    @pl.when(has_slow)
    def _():
        pl.semaphore_signal(barrier, inc=1, device_id={"grid": slow_id})

    pl.semaphore_signal(barrier, inc=1, device_id={"grid": fast_id})
    for slot in (1, 2):
        pl.semaphore_signal(barrier, inc=1, device_id={"orb": quarters[slot]})

    half = REACH // 2
    lead = [REACH - 1, REACH - 2]
    rest = list(range(REACH - 2))
    first_group = list(range(REACH - late))
    arrivals = (
        [first_group] + [[k] for k in range(REACH - late, REACH)],
        [[*lead, 0]] + [[k] for k in rest[1:]],
        [[*lead, 0]] + [[k] for k in rest[1:]],
    )

    before = [sum(len(group) for group in arrivals[:r]) for r in range(3)]

    def at(d):
        return d + odd * (planes - 1 - 2 * d)

    def span(d, count):
        return pl.ds(d + odd * (planes - count - 2 * d), count)

    def meet(i):
        reach = 2 ** i
        for peer in (g - reach, g + reach):
            @pl.when(jnp.logical_and(peer >= 0, peer < n))
            def _():
                pl.semaphore_signal(met.at[i], inc=1, device_id={"grid": peer})

    def met_by(i):
        reach = 2 ** i
        pl.semaphore_wait(
            met.at[i], jnp.where(g >= reach, 1, 0) + jnp.where(g + reach < n, 1, 0))

    rounds = met.shape[0] - 1

    order = list(range(REACH)) + list(range(planes - 1, REACH - 1, -1))
    groups = [(d, 2) for d in range(0, REACH, 2)]
    groups += [(planes - half, half), (REACH, planes - REACH - half)]

    def load(i):
        piece = span(*groups[i])
        return [
            pltpu.make_async_copy(hbm.at[piece], ref.at[piece], ld_sem.at[i])
            for hbm, ref in ((orb_hbm, orb), (tri_hbm, tri))
        ]

    def loaded(d):
        for i, (low, count) in enumerate(groups):
            if d == (low if low < REACH else low + count - 1):
                piece = pl.ds(0, 2 * count)
                pltpu.make_async_copy(orb_hbm.at[piece], orb.at[piece], ld_sem.at[i]).wait()

    for i in range(len(groups)):
        for copy in load(i):
            copy.start()
    mats = [
        pltpu.make_async_copy(pot_hbm, pot, mat_sem.at[0]),
        pltpu.make_async_copy(eig_hbm, eig, mat_sem.at[1]),
        pltpu.make_async_copy(freq_hbm, freq, mat_sem.at[2]),
    ]
    for copy in mats:
        copy.start()

    fields = (src, img, two)

    def slow(r, k):
        group = [i for i, ks in enumerate(arrivals[r]) if k in ks][0]
        return pltpu.make_async_remote_copy(
            src_ref=fields[r].at[at(k)], dst_ref=hslow.at[r, k],
            send_sem=slow_s.at[min(r, 1)], recv_sem=slow_r.at[before[r] + group],
            device_id={"grid": slow_id}, device_id_type=pl.DeviceIdType.MESH)

    def slow_wait(r, ks):
        group = arrivals[r].index(ks)
        piece = hslow.at[r, pl.ds(0, len(ks))]
        pltpu.make_async_remote_copy(
            src_ref=piece, dst_ref=piece,
            send_sem=slow_s.at[min(r, 1)], recv_sem=slow_r.at[before[r] + group],
            device_id={"grid": slow_id}, device_id_type=pl.DeviceIdType.MESH).wait_recv()

    def sent(low, count, buffer, sem):
        piece = buffer.at[pl.ds(low, count)]
        pltpu.make_async_remote_copy(
            src_ref=piece, dst_ref=piece, send_sem=sem, recv_sem=slow_r.at[0],
            device_id={"grid": fast_id}, device_id_type=pl.DeviceIdType.MESH).wait_send()

    def fast(r, i):
        return pltpu.make_async_remote_copy(
            src_ref=fields[r].at[span(planes - half * (i + 1), half)],
            dst_ref=hfast.at[r, pl.ds(half * (1 - i) + odd * half * (2 * i - 1), half)],
            send_sem=fast_s.at[min(r, 1)], recv_sem=fast_r.at[i],
            device_id={"grid": fast_id}, device_id_type=pl.DeviceIdType.MESH)

    def fast_both(r):
        return pltpu.make_async_remote_copy(
            src_ref=fields[r].at[span(planes - REACH, REACH)], dst_ref=hfast.at[r],
            send_sem=fast_s.at[1], recv_sem=fast_r.at[1 + r],
            device_id={"grid": fast_id}, device_id_type=pl.DeviceIdType.MESH)

    def send(r, *ks):
        @pl.when(has_slow)
        def _():
            for k in ks:
                slow(r, k).start()

    def rows_in(slot):
        return pl.ds(pl.multiple_of(quarters[slot] * quarter, 8), quarter)

    def rows_of(s, count):
        return pl.ds(pl.multiple_of(s * count, count), count)

    def over(step, init, count=wide):
        return lax.fori_loop(0, ny // count, step, init)

    def ship_copy(field, slot, d, count):
        piece = pl.ds(d - late, count)
        return pltpu.make_async_remote_copy(
            src_ref=ship.at[field, slot, piece], dst_ref=land.at[field, slot, piece],
            send_sem=ship_s, recv_sem=ship_r.at[field],
            device_id={"orb": quarters[slot]}, device_id_type=pl.DeviceIdType.MESH)

    def ship_wait(field):
        pltpu.make_async_remote_copy(
            src_ref=ship.at[field], dst_ref=land.at[field],
            send_sem=ship_s, recv_sem=ship_r.at[field],
            device_id={"orb": both}, device_id_type=pl.DeviceIdType.MESH).wait_recv()

    cut = 2 * REACH - half
    batches = (
        (
            (REACH, 1), (REACH + 1, half - 1), (REACH + half, planes - REACH - half),
            (late, REACH - late),
        ),
        ((2 * REACH - 1, planes - 2 * REACH + 1),)
        + tuple((d, 1) for d in range(2 * REACH - 2, cut - 1, -1))
        + ((REACH, cut - REACH),)
        + tuple((d, 1) for d in range(REACH - 1, late - 1, -1)),
    )

    def share(field, value, batch):
        d, count = batches[field][batch]
        for slot in range(3):
            rows = rows_in(slot)
            for e in range(d, d + count):
                ship[field, slot, e - late] = orb[at(e), rows, :] * value[at(e), rows, :]
            ship_copy(field, slot, d, count).start()

    zero = jnp.zeros((wide, nz), jnp.float32)

    def arrive(r, ks, acc):
        @pl.when(has_slow)
        def _():
            slow_wait(r, ks)

            def step(s, carry):
                rows = rows_of(s, wide)
                values = [hslow[r, k, rows, :] for k in ks]
                for d in range(REACH):
                    terms = [COEFS[d + 1 + k] * v for k, v in zip(ks, values) if d + k < REACH]
                    if terms:
                        acc[at(d), rows, :] = acc[at(d), rows, :] + functools.reduce(jnp.add, terms)
                return carry

            over(step, 0)

    def square_of(ref, d, total):
        def step(s, carry):
            value = ref[at(d), rows_of(s, wide), :]
            return carry + value * value

        return over(step, total)

    def across(value, out, low, high):
        def plane(d):
            p = at(d)
            whole = value[p]
            high_part = whole.astype(jnp.bfloat16)
            low_part = (whole - high_part.astype(jnp.float32)).astype(jnp.bfloat16)
            product = functools.partial(jnp.dot, preferred_element_type=jnp.float32)
            along_z = product(high_part, cz[0]) + product(low_part, cz[0]) + product(high_part, cz[1])
            along_y = product(cy[0], high_part) + product(cy[0], low_part) + product(cy[1], high_part)
            out[p] = along_z + along_y

        count = high - low
        size = max(k for k in range(1, REACH + 1) if count % k == 0)

        def group(i, carry):
            for j in range(size):
                plane(low + i * size + j)
            return carry

        lax.fori_loop(0, count // size, group, 0)

    def along(r, value, out, low, high):
        for side in (0, 1):
            @pl.when(odd == side)
            def _(side=side):
                def place(d):
                    return planes - 1 - d if side else d

                def part(d, rows):
                    if d < planes:
                        return value[place(d), rows, :]
                    k = d - planes
                    return hfast[r, REACH - 1 - k if side else k, rows, :]

                def strip(s, carry):
                    rows = rows_of(s, STRIP)
                    parts = {
                        d: part(d, rows)
                        for d in range(max(0, low - REACH), min(planes, high) + REACH)
                        if d < high + REACH
                    }
                    for d in range(low, high):
                        here = out.at[place(d), rows, :]
                        total = here[...] + (pot[place(d), rows, :] + (3.0 * COEFS[0] - energy)) * parts[d]
                        for k in range(1, REACH + 1):
                            near = [parts[e] for e in (d - k, d + k) if e in parts]
                            total = total + COEFS[k] * (near[0] + near[1] if len(near) == 2 else near[0])
                        here[...] = total
                    return carry

                over(strip, 0, STRIP)

    def fold(total):
        total = functools.reduce(
            lambda a, b: a + b, [total[i:i + 8] for i in range(0, wide, 8)])
        total = functools.reduce(
            lambda a, b: a + b, [total[:, i:i + 128] for i in range(0, nz, 128)])
        return jnp.sum(total, axis=0, keepdims=True)

    def exchange(r, j, slot):
        return pltpu.make_async_remote_copy(
            src_ref=sums.at[r, slot], dst_ref=sums.at[r, slot],
            send_sem=sum_s, recv_sem=sum_r.at[r],
            device_id={"grid": lax.rem(g + j, n)}, device_id_type=pl.DeviceIdType.MESH)

    def exchanged(r):
        return pltpu.make_async_remote_copy(
            src_ref=sums.at[r, pl.ds(0, n - 1)], dst_ref=sums.at[r, pl.ds(0, n - 1)],
            send_sem=sum_s, recv_sem=sum_r.at[r],
            device_id={"grid": fast_id}, device_id_type=pl.DeviceIdType.MESH)

    def post(r, *totals):
        for i in range(2):
            row = fold(totals[i]) if i < len(totals) else jnp.zeros((1, 128), jnp.float32)
            sums[r, g, i:i + 1, :] = row
        for j in range(1, n):
            exchange(r, j, g).start()

    def collect(r):
        exchanged(r).wait_recv()
        total = sums[r, 0]
        for m in range(1, n):
            total = total + sums[r, m]
        return tuple(jnp.sum(total[i:i + 1], keepdims=True) for i in range(2))

    def spread(value):
        return jnp.broadcast_to(value, (1, nz))

    circulant(cz, 32)
    circulant(cy, 32)

    total_src = zero
    for d in order:
        loaded(d)

        def step(s, carry, d=d):
            rows = rows_of(s, wide)
            value = orb[at(d), rows, :] * tri[at(d), rows, :]
            src[at(d), rows, :] = value
            return carry + value * value

        total_src = over(step, total_src)
        if d == order[0]:
            pl.semaphore_wait(barrier, 3 + has_slow.astype(jnp.int32))
            pl.semaphore_signal(met.at[rounds], inc=1, device_id={"orb": first})
            meet(0)
        if d < REACH:
            send(0, d)
        if d == planes - half:
            fast(0, 0).start()
        if d == planes - REACH:
            fast(0, 1).start()
    for copy in mats:
        copy.wait()
    energy = eig[0]
    squared = freq[0] * freq[0]

    across(src, img, REACH, REACH + 1)
    fast(0, 0).wait_recv()
    along(0, src, img, REACH, REACH + 1)
    pl.semaphore_wait(met.at[rounds], 1)
    share(0, img, 0)
    across(src, img, REACH + 1, REACH + half)
    along(0, src, img, REACH + 1, REACH + half)
    share(0, img, 1)
    across(src, img, REACH + half, planes)
    if rounds > 1:
        met_by(0)
        meet(1)
    fast(0, 1).wait_recv()
    along(0, src, img, REACH + half, planes)
    fast_both(1).start()
    share(0, img, 2)
    across(src, img, 0, REACH)
    along(0, src, img, 0, REACH)
    for i in range(1, rounds - 1):
        met_by(i)
        meet(i + 1)
    total_img = zero
    for d in range(REACH, planes):
        total_img = square_of(img, d, total_img)
    early = list(range(REACH - late))
    arrive(0, early, img)
    send(1, *lead)
    share(0, img, 3)
    for k in early:
        total_img = square_of(img, REACH - 1 - k, total_img)
    across(img, two, late, planes)
    for k in range(REACH - late, REACH):
        arrive(0, [k], img)
        total_img = square_of(img, REACH - 1 - k, total_img)
        if k < REACH - 1:
            across(img, two, REACH - 1 - k, REACH - k)
    met_by(rounds - 1)
    post(0, total_src, total_img)
    send(1, *rest)
    across(img, two, 0, 1)
    fast_both(1).wait_recv()
    along(1, img, two, 0, planes)
    fast_both(2).start()

    across(two, fin, REACH, planes)
    fast_both(2).wait_recv()
    arrive(1, [*lead, 0], two)
    send(2, REACH - 1)
    across(two, fin, REACH - 1, REACH)
    along(2, two, fin, 2 * REACH - 1, planes)
    share(1, fin, 0)
    norm0, form0 = collect(0)
    step0 = norm0 / (form0 + squared * norm0)
    back = spread(1.0 - step0 * squared)
    step0_row = spread(step0)

    def square_res(d, total):
        def step(s, carry):
            rows = rows_of(s, wide)
            value = back * src[at(d), rows, :] - step0_row * two[at(d), rows, :]
            return carry + value * value

        return over(step, total)

    total_res = zero
    for d in range(REACH - 1, planes):
        total_res = square_res(d, total_res)
    for k in range(1, half):
        arrive(1, [k], two)
        d = REACH - 1 - k
        if d in lead:
            send(2, d)
        across(two, fin, d, d + 1)
        along(2, two, fin, REACH + d, REACH + d + 1)
        share(1, fin, k)
        total_res = square_res(d, total_res)
    for k in range(half, rest[-1] + 1):
        arrive(1, [k], two)
    for d in range(half):
        total_res = square_res(d, total_res)
    post(1, total_res)
    send(2, *rest)
    across(two, fin, 0, half)
    along(2, two, fin, 0, cut)
    share(1, fin, half)
    arrive(2, [*lead, 0], fin)
    share(1, fin, half + 1)

    norm1, _ = collect(1)
    ratio = norm1 / norm0
    keep = 1.0 - step0 * squared + ratio
    keep_row = spread(keep)

    def square_dir(d, total):
        def step(s, carry):
            rows = rows_of(s, wide)
            value = keep_row * src[at(d), rows, :] - step0_row * two[at(d), rows, :]
            return carry + value * value

        return over(step, total)

    def square_fin(d, total):
        def step(s, carry):
            rows = rows_of(s, wide)
            value = keep_row * img[at(d), rows, :] - step0_row * fin[at(d), rows, :]
            return carry + value * value

        return over(step, total)

    def loop_over(low, high, body, total):
        return lax.fori_loop(low, high, body, total)

    total_dir = loop_over(0, planes, square_dir, zero)
    total_fin = loop_over(REACH - 1, planes, square_fin, zero)
    for k in rest[1:]:
        arrive(2, [k], fin)
        d = REACH - 1 - k
        if k < rest[-1]:
            share(1, fin, half + 1 + k)
            total_fin = square_fin(d, total_fin)
    for d in range(REACH - rest[-1]):
        total_fin = square_fin(d, total_fin)
    post(2, total_dir, total_fin)
    for k in range(rest[-1], REACH - late):
        share(1, fin, half + 1 + k)
    form_dir, form_fin = collect(2)
    step1 = norm1 / (form_fin + squared * form_dir)

    near_img = -4.0 * (step0 + step1 * keep)
    near_fin = 4.0 * (step1 * step0)
    mix[3, 0:1, :] = spread(near_img)
    mix[3, 1:2, :] = spread(near_fin)

    def tell(slot):
        return pltpu.make_async_remote_copy(
            src_ref=mix.at[3], dst_ref=mix.at[slot],
            send_sem=mix_s, recv_sem=mix_r,
            device_id={"orb": quarters[slot]}, device_id_type=pl.DeviceIdType.MESH)

    near_img_row = spread(near_img)
    near_fin_row = spread(near_fin)

    def respond(slot, d):
        rows = rows_in(slot)
        return orb[at(d), rows, :] * (
            near_img_row * img[at(d), rows, :] + near_fin_row * fin[at(d), rows, :])

    def all_of(source, target, send, recv):
        return pltpu.make_async_remote_copy(
            src_ref=source, dst_ref=target, send_sem=send, recv_sem=recv,
            device_id={"orb": both}, device_id_type=pl.DeviceIdType.MESH)

    told = all_of(mix.at[pl.ds(0, 3)], mix.at[pl.ds(0, 3)], mix_s, mix_r)
    late_all = all_of(ship_late, land_late, late_s, late_r)

    def late_copy(slot):
        return pltpu.make_async_remote_copy(
            src_ref=ship_late.at[slot], dst_ref=land_late.at[slot],
            send_sem=late_s, recv_sem=late_r,
            device_id={"orb": quarters[slot]}, device_id_type=pl.DeviceIdType.MESH)

    for slot in range(3):
        for d in range(late):
            ship_late[slot, d] = respond(slot, d)
        tell(slot).start()
        late_copy(slot).start()

    @pl.when(has_slow)
    def _():
        sent(0, 1, hslow, slow_s.at[0])

    sent(0, 1, hfast, fast_s.at[0])
    sol_src = spread(step0 + step1 * keep)
    sol_two = spread(step1 * step0)

    def solve(p, carry):
        def step(s, inner):
            rows = rows_of(s, wide)
            src[p, rows, :] = sol_src * src[p, rows, :] - sol_two * two[p, rows, :]
            return inner

        return over(step, carry)

    lax.fori_loop(0, planes, solve, 0)
    for d in range(planes):
        dens[at(d)] = respond(3, d)
    told.wait_recv()
    for field in range(2):
        ship_wait(field)
    for e in range(late, planes):
        total = dens[at(e)]
        for slot in range(3):
            for field in range(2):
                total = total + mix[slot, field:field + 1, :] * land[field, slot, e - late]
        dens[at(e)] = total
    late_all.wait_recv()
    for d in range(late):
        dens[at(d)] = dens[at(d)] + (land_late[0, d] + land_late[1, d] + land_late[2, d])

    @pl.when(has_slow)
    def _():
        sent(1, 2, hslow, slow_s.at[1])

    sent(1, 2, hfast, fast_s.at[1])
    all_of(
        sums.at[pl.ds(0, 3), pl.ds(0, n - 1)], sums.at[pl.ds(0, 3), pl.ds(0, n - 1)],
        sum_s, sum_r.at[0]).wait_send()
    all_of(ship, land, ship_s, ship_r.at[0]).wait_send()
    told.wait_send()
    late_all.wait_send()


def write_out(sol, den, sol_hbm, den_hbm, sem):
    planes = sol.shape[0]
    cuts = [planes * i // 4 for i in range(5)]
    copies = [
        pltpu.make_async_copy(sol.at[pl.ds(a, b - a)], sol_hbm.at[pl.ds(a, b - a)], sem.at[i])
        for i, (a, b) in enumerate(zip(cuts, cuts[1:]))
    ]
    copies.append(pltpu.make_async_copy(den, den_hbm, sem.at[4]))
    for copy in copies:
        copy.start()
    for copy in copies:
        copy.wait()


def body(n, groups, orbitals, potential, trial_potential, eigenvalues, frequency):
    count, planes, ny, nz = orbitals.shape
    assert count == 1 and groups == 4 and n % 2 == 0
    assert planes >= 2 * REACH
    assert ny % 32 == 0 and nz % 128 == 0 and min(ny, nz) > 2 * REACH
    quarter = ny // groups
    late = REACH // 3
    early = planes - late
    f32 = jnp.float32
    field = pltpu.VMEM((planes, ny, nz), f32)
    dma = pltpu.SemaphoreType.DMA
    anywhere = pl.BlockSpec(memory_space=pl.ANY)
    hbm = pl.BlockSpec(memory_space=pltpu.HBM)
    vmem = pl.BlockSpec(memory_space=pltpu.VMEM)
    sol, den = pl.pallas_call(
        functools.partial(kernel, n),
        out_shape=(
            pltpu.VMEM((planes, ny, nz), f32),
            pltpu.VMEM((planes, quarter, nz), f32),
        ),
        in_specs=[hbm] * 5,
        out_specs=(vmem, vmem),
        scratch_shapes=[field] * 6 + [
            pltpu.VMEM((2, nz, nz), jnp.bfloat16),
            pltpu.VMEM((2, ny, ny), jnp.bfloat16),
            pltpu.VMEM((3, REACH, ny, nz), f32),
            pltpu.VMEM((3, REACH, ny, nz), f32),
            pltpu.VMEM((3, n, 2, 128), f32),
            pltpu.VMEM((2, 3, early, quarter, nz), f32),
            pltpu.VMEM((2, 3, early, quarter, nz), f32),
            pltpu.VMEM((3, late, quarter, nz), f32),
            pltpu.VMEM((3, late, quarter, nz), f32),
            pltpu.VMEM((4, 2, nz), f32),
            pltpu.SMEM((1,), f32), pltpu.SMEM((1,), f32),
            pltpu.SemaphoreType.REGULAR(((n - 1).bit_length() + 1,)),
            dma((2 + REACH // 2,)), dma((3,)),
            dma((2,)), dma((1 + late + 2 * (REACH - 2),)), dma((2,)), dma((4,)), dma(()), dma((3,)),
            dma(()), dma((2,)), dma(()), dma(()), dma(()), dma(()),
        ],
        compiler_params=pltpu.CompilerParams(
            collective_id=0, has_side_effects=True, vmem_limit_bytes=50 * 2**20),
        name="sternheimer",
    )(
        orbitals.reshape(planes, ny, nz), potential, trial_potential,
        eigenvalues, frequency,
    )
    sol, den = pl.pallas_call(
        write_out,
        out_shape=(jax.ShapeDtypeStruct(sol.shape, f32), jax.ShapeDtypeStruct(den.shape, f32)),
        in_specs=[vmem] * 2,
        out_specs=(anywhere, anywhere),
        scratch_shapes=[dma((5,))],
        compiler_params=pltpu.CompilerParams(vmem_limit_bytes=2**20),
        name="write_out",
    )(sol, den)
    return sol.reshape(orbitals.shape), den


def solution(mesh):
    in_specs = (
        P("orb", "grid", None, None),
        P("grid", None, None),
        P("grid", None, None),
        P("orb"),
        P(),
    )
    out_specs = (P("orb", "grid", None, None), P("grid", "orb", None))
    call = functools.partial(body, mesh.shape["grid"], mesh.shape["orb"])
    return jax.shard_map(call, mesh=mesh, in_specs=in_specs, out_specs=out_specs, check_vma=False)
```
